32 devices in a mesh: seq: 16 (over z, y, core), tp: 2 (over x).
Axes of the slice: x: 2, y: 2, z: 4, core: 2. Of those that a mesh axis runs over, the one named last changes fastest.
Arguments:
- queries: bfloat16 [16384, 2048], P('seq', 'tp'), may hold values from -6 to 6
- keys: bfloat16 [16384, 2048], P('seq', 'tp'), may hold values from -6 to 6
- values: bfloat16 [16384, 2048], P('seq', 'tp'), may hold values from -6 to 6
- saved_output: bfloat16 [16384, 2048], P('seq', 'tp'), may hold values from -2 to 2
- grad_output: bfloat16 [16384, 2048], P('seq', 'tp'), may hold values from -6 to 6
- log_norm: float32 [16, 16384], P('tp', 'seq'), as said below
- global_keys: bfloat16 [16, 128, 2048], P('seq', None, 'tp'), may hold values from -6 to 6
- global_values: bfloat16 [16, 128, 2048], P('seq', None, 'tp'), may hold values from -6 to 6
- flow_links: int32 [128, 3], replicated, may hold values from 0 to 127, as said below
- glob_owner: int32 [128], replicated, may hold values from 0 to 15
Outputs:
- grad_queries: bfloat16 [16384, 2048], P('seq', 'tp')
- grad_keys: bfloat16 [16384, 2048], P('seq', 'tp')
- grad_values: bfloat16 [16384, 2048], P('seq', 'tp')
- grad_global_keys: bfloat16 [128, 2048], P(None, 'tp')
- grad_global_values: bfloat16 [128, 2048], P(None, 'tp')
The draws below stay inside these ranges and needn't reach their ends.
Inputs may be any that keep to these rules, and one draw needn't show every extreme that they name: `flow_links`: the 24 entries of the query blocks of one index of seq name blocks held by any one index of seq at most 2 times, and on every index some holder is named exactly 2 times. `log_norm`: each entry lies within 1 of log(896) + 0.5.
All inputs are finite; a program needn't handle non-finite values.
Results may differ from the reference program's by a relative error of at most 0.0068.
Values may be sent and summed in bfloat16 or wider, within the bound.
No kernel may reach another device: no remote copies, remote signals or barrier semaphores. Data moves between devices by JAX's collectives and lax.ppermute only.
A program may use at most 256 MiB of HBM per device.

```python
import math
import jax
import jax.numpy as jnp
from jax import lax

HD = 128
HEADS = 16
BLK = 128
R = 3
G = 128
BLK_DEV = 8
NBLK = 128
TOKENS = 16384
FEAT = 2048
N_SEQ = 16


def draw_flow_links(key, part):
    entries = BLK_DEV * R
    capacity = max(2, (entries + N_SEQ - 1) // N_SEQ)
    pool = jnp.arange(N_SEQ * capacity, dtype=jnp.int32) // capacity

    def one_device(device_key):
        first_key, second_key, third_key, fourth_key = jax.random.split(device_key, 4)
        rest = jax.random.permutation(first_key, pool[capacity:])
        chosen = jnp.concatenate([pool[:capacity], rest])[:entries]
        relabel = jax.random.permutation(second_key, jnp.arange(N_SEQ, dtype=jnp.int32))
        target = relabel[chosen]
        target = target[jax.random.permutation(third_key, jnp.arange(entries, dtype=jnp.int32))]
        inside = jax.random.randint(fourth_key, (entries,), 0, BLK_DEV, dtype=jnp.int32)
        return target * BLK_DEV + inside
    device_keys = jax.random.split(jax.random.fold_in(key, 7), N_SEQ)
    return jax.vmap(one_device)(device_keys).reshape(N_SEQ * BLK_DEV, R).astype(jnp.int32)


def draw_log_norm(key, part):
    center = math.log((3 + R) * BLK + G) + 0.5
    noise_key = jax.random.fold_in(key, 11)
    noise = jax.random.uniform(noise_key, (HEADS, TOKENS), jnp.float32, -0.5, 0.5)
    return (center + noise).astype(jnp.float32)


def set_ends(result, rng, smallest, largest):
    shape = result.shape
    spot = [jax.random.randint(jax.random.fold_in(rng, axis), (), 0, shape[axis]) for axis in range(len(shape))]
    result = result.at[tuple(spot)].set(smallest)
    longest = shape.index(max(shape))
    spot[longest] = (spot[longest] + 1) % shape[longest]
    return result.at[tuple(spot)].set(largest)


def shard_levels(key, dims, shards, least, largest):
    def one(dim, blocks):
        heights = jax.random.uniform(jax.random.fold_in(jax.random.fold_in(key, 6), dim), (blocks,), jnp.float32, least / len(shards), largest / len(shards))
        return jnp.repeat(jnp.exp(heights), dims[dim] // blocks).reshape((-1,) + (1,) * (len(dims) - dim - 1))

    factor_of = one(*shards[0])
    for cut in shards[1:]:
        factor_of = factor_of * one(*cut)
    return factor_of


def scatter_about(own_key, extent, deviation, most, shards=(), held_as=jnp.bfloat16):
    values = deviation * jax.random.normal(own_key, extent, jnp.float32)
    if shards:
        values = values * shard_levels(own_key, extent, shards, -0.22, 0.18)
    return jnp.clip(values, -most, most).astype(held_as)


def setup_inputs(seed: int = 0) -> dict:
    seeds = jax.random.split(jax.random.key(seed), 11)
    queries = scatter_about(seeds[0], (TOKENS, FEAT), 1.0, 6.0, ((0, 16), (1, 2)))
    keys = scatter_about(seeds[1], (TOKENS, FEAT), 1.0, 6.0, ((0, 16), (1, 2)))
    values = scatter_about(seeds[2], (TOKENS, FEAT), 1.0, 6.0, ((0, 16), (1, 2)))
    saved_output = scatter_about(seeds[3], (TOKENS, FEAT), 0.3, 2.0, ((0, 16), (1, 2)))
    grad_output = scatter_about(seeds[4], (TOKENS, FEAT), 1.0, 6.0, ((0, 16), (1, 2)))
    log_norm = draw_log_norm(jax.random.fold_in(seeds[10], 71), 0)
    global_keys = scatter_about(seeds[6], (N_SEQ, G, FEAT), 1.0, 6.0, ((0, 16), (2, 2)))
    global_values = scatter_about(seeds[7], (N_SEQ, G, FEAT), 1.0, 6.0, ((0, 16), (2, 2)))
    flow_links = draw_flow_links(jax.random.fold_in(seeds[10], 71), 0)
    glob_owner = set_ends(jax.random.randint(seeds[9], (G,), 0, N_SEQ), jax.random.fold_in(seeds[9], 1), 0, N_SEQ - 1).astype(jnp.int32)
    return {"queries": queries, "keys": keys, "values": values, "saved_output": saved_output, "grad_output": grad_output, "log_norm": log_norm, "global_keys": global_keys, "global_values": global_values, "flow_links": flow_links, "glob_owner": glob_owner}


def low_round(value):
    return lax.optimization_barrier(value.astype(jnp.bfloat16)).astype(jnp.float32)


def pair_terms(query_rows, grad_rows, norm_rows, delta_rows, key_rows, value_rows, factor):
    query_full = query_rows.astype(jnp.float32)
    grad_full = grad_rows.astype(jnp.float32)
    key_full = key_rows.astype(jnp.float32)
    value_full = value_rows.astype(jnp.float32)
    scores = jnp.einsum("qhd,khd->hqk", query_full, key_full) * factor
    attend = jnp.exp(scores - norm_rows[:, :, None])
    grad_attend = jnp.einsum("qhd,khd->hqk", grad_full, value_full)
    grad_scores = attend * (grad_attend - delta_rows[:, :, None])
    attend_low = low_round(attend)
    scores_low = low_round(grad_scores)
    grad_q = factor * jnp.einsum("hqk,khd->qhd", scores_low, key_full)
    grad_k = factor * jnp.einsum("hqk,qhd->khd", scores_low, query_full)
    grad_v = jnp.einsum("hqk,qhd->khd", attend_low, grad_full)
    return grad_q, grad_k, grad_v


def reference(queries, keys, values, saved_output, grad_output, log_norm, global_keys, global_values, flow_links, glob_owner):
    factor = HD ** -0.5
    shape_blocks = (NBLK, BLK, HEADS, HD)
    query_blocks = queries.reshape(shape_blocks)
    key_blocks = keys.reshape(shape_blocks)
    value_blocks = values.reshape(shape_blocks)
    grad_blocks = grad_output.reshape(shape_blocks)
    product = grad_output.astype(jnp.float32) * saved_output.astype(jnp.float32)
    delta_blocks = jnp.transpose(jnp.sum(product.reshape(shape_blocks), axis=3), (0, 2, 1))
    norm_blocks = jnp.transpose(log_norm.reshape(HEADS, NBLK, BLK), (1, 0, 2))
    token_order = jnp.arange(G, dtype=jnp.int32)
    owners = glob_owner.astype(jnp.int32)
    glob_key_now = global_keys[owners, token_order].reshape(G, HEADS, HD)
    glob_val_now = global_values[owners, token_order].reshape(G, HEADS, HD)

    def step(carry, block):
        key_acc, value_acc, glob_key_acc, glob_val_acc = carry
        window = jnp.stack([(block + NBLK - 1) % NBLK, block, (block + 1) % NBLK]).astype(jnp.int32)
        query_here = query_blocks[block]
        grad_here = grad_blocks[block]
        norm_here = norm_blocks[block]
        delta_here = delta_blocks[block]
        win_keys = key_blocks[window].reshape(3 * BLK, HEADS, HD)
        win_vals = value_blocks[window].reshape(3 * BLK, HEADS, HD)
        dq_win, dk_win, dv_win = pair_terms(query_here, grad_here, norm_here, delta_here, win_keys, win_vals, factor)
        dq_glob, dk_glob, dv_glob = pair_terms(query_here, grad_here, norm_here, delta_here, glob_key_now, glob_val_now, factor)
        linked = flow_links[block].astype(jnp.int32)

        def one_link(key_one, value_one):
            return pair_terms(query_here, grad_here, norm_here, delta_here, key_one, value_one, factor)

        dq_link, dk_link, dv_link = jax.vmap(one_link)(key_blocks[linked], value_blocks[linked])
        total_q = dq_win + dq_glob + jnp.sum(low_round(dq_link), axis=0)
        key_acc = key_acc.at[window].add(dk_win.reshape(3, BLK, HEADS, HD))
        key_acc = key_acc.at[linked].add(low_round(dk_link))
        value_acc = value_acc.at[window].add(dv_win.reshape(3, BLK, HEADS, HD))
        value_acc = value_acc.at[linked].add(low_round(dv_link))
        glob_key_acc = glob_key_acc + dk_glob
        glob_val_acc = glob_val_acc + dv_glob
        return (key_acc, value_acc, glob_key_acc, glob_val_acc), total_q.astype(jnp.bfloat16)

    start = (jnp.zeros(shape_blocks, jnp.float32), jnp.zeros(shape_blocks, jnp.float32),
             jnp.zeros((G, HEADS, HD), jnp.float32), jnp.zeros((G, HEADS, HD), jnp.float32))
    final, grad_q_blocks = lax.scan(step, start, jnp.arange(NBLK, dtype=jnp.int32))
    key_acc, value_acc, glob_key_acc, glob_val_acc = final
    grad_queries = grad_q_blocks.reshape(TOKENS, FEAT)
    grad_keys = key_acc.astype(jnp.bfloat16).reshape(TOKENS, FEAT)
    grad_values = value_acc.astype(jnp.bfloat16).reshape(TOKENS, FEAT)
    grad_global_keys = glob_key_acc.astype(jnp.bfloat16).reshape(G, FEAT)
    grad_global_values = glob_val_acc.astype(jnp.bfloat16).reshape(G, FEAT)
    return (grad_queries, grad_keys, grad_values, grad_global_keys, grad_global_values)
```

```python
import functools
import math

import jax
import jax.numpy as jnp
from jax import lax
from jax.experimental import pallas as pl
from jax.experimental.pallas import tpu as pltpu
from jax.sharding import PartitionSpec as P

HD = 128
BLK = 128
R = 3
G = 128
W = 3
FACTOR = HD ** (-0.5)
LOG2E = math.log2(math.e)
STAGE = 4


def pair_kernel(left_ref, right_ref, out_ref):
    heads = out_ref.shape[0]
    for head in range(heads):
        cols = slice(head * HD, (head + 1) * HD)
        out_ref[head, 0, :, :HD] = left_ref[:, cols]
        out_ref[head, 0, :, HD:] = right_ref[:, cols]


def pair_heads(left, right, share):
    tokens, features = left.shape
    heads = features // HD
    part = tokens // share
    rows = min(256, part)
    steps = part // rows
    out = pl.pallas_call(
        pair_kernel,
        grid=(share, steps),
        in_specs=[pl.BlockSpec((rows, features), lambda s, t: (s * steps + t, 0))] * 2,
        out_specs=pl.BlockSpec((heads, 1, rows, 2 * HD), lambda s, t: (0, s, t, 0)),
        out_shape=jax.ShapeDtypeStruct((heads, share, part, 2 * HD), left.dtype),
        cost_estimate=pl.CostEstimate(
            flops=0, bytes_accessed=4 * tokens * features * 2, transcendentals=0
        ),
    )(left, right)
    return out.reshape(heads * share, part, 2 * HD)


def unpair_kernel(in_ref, *out_refs):
    heads = in_ref.shape[0]
    for head in range(heads):
        cols = slice(head * HD, (head + 1) * HD)
        for which, out_ref in enumerate(out_refs):
            out_ref[:, cols] = in_ref[head, 0, :, which * HD : (which + 1) * HD]


def unpair_heads(mixed, share):
    parts, part, width = mixed.shape
    heads = parts // share
    count = width // HD
    rows = min(256, part)
    steps = part // rows
    shape = jax.ShapeDtypeStruct((share * part, heads * HD), mixed.dtype)
    return pl.pallas_call(
        unpair_kernel,
        grid=(share, steps),
        in_specs=[pl.BlockSpec((heads, 1, rows, width), lambda s, t: (0, s, t, 0))],
        out_specs=[pl.BlockSpec((rows, heads * HD), lambda s, t: (s * steps + t, 0))] * count,
        out_shape=[shape] * count,
        cost_estimate=pl.CostEstimate(
            flops=0, bytes_accessed=4 * parts * part * width, transcendentals=0
        ),
    )(mixed.reshape(heads, share, part, width))


def attention_kernel(
    table_ref, stats_ref, pair_ref, kv_ref, glob_ref, dq_ref, dkv_ref, dglob_ref, acc, stage, sems
):
    count, tile, _ = pair_ref.shape
    total = acc.shape[0]
    kinds = (W + R) * (BLK // tile)

    def clear(block, carry):
        acc[block] = jnp.zeros((tile, 2 * HD), jnp.float32)
        return carry

    lax.fori_loop(0, total, clear, 0)
    dglob_ref[...] = jnp.zeros_like(dglob_ref)
    zero = jnp.zeros((tile, HD), jnp.bfloat16)

    def one_block(block, carry):
        pair = pair_ref[block]
        mixed = jnp.concatenate(
            [
                jnp.concatenate([pair[:, :HD], zero], axis=1),
                jnp.concatenate([zero, pair[:, HD:]], axis=1),
            ],
            axis=0,
        )
        stats = stats_ref[block]
        norm = stats[0:1] * LOG2E
        delta = stats[1:2]
        places = [table_ref[block * kinds + kind] for kind in range(kinds)]
        rows = jnp.concatenate([kv_ref[place] for place in places] + [glob_ref[...]], axis=0)
        both = lax.dot_general(
            rows, mixed, (((1,), (1,)), ((), ())), preferred_element_type=jnp.float32
        )
        attend = jnp.exp2(both[:, :tile] * (FACTOR * LOG2E) - norm)
        grad_scores = attend * (both[:, tile:] - delta)
        attend_low = attend.astype(jnp.bfloat16)
        scores_low = grad_scores.astype(jnp.bfloat16)
        grad_kv = jnp.dot(
            jnp.concatenate([scores_low, attend_low], axis=1),
            mixed,
            preferred_element_type=jnp.float32,
        )
        for kind, place in enumerate(places):
            acc[place] += grad_kv[kind * tile : (kind + 1) * tile]
        dglob_ref[...] += grad_kv[kinds * tile :]
        grad_q = lax.dot_general(
            scores_low, rows[:, :HD], (((0,), (0,)), ((), ())), preferred_element_type=jnp.float32
        )
        dq_ref[block] = (grad_q * FACTOR).astype(jnp.bfloat16)
        return carry

    lax.fori_loop(0, count, one_block, 0)
    dglob_ref[:, :HD] = dglob_ref[:, :HD] * FACTOR

    def copy_out(step, slot):
        return pltpu.make_async_copy(
            stage.at[slot], dkv_ref.at[pl.ds(step * STAGE, STAGE)], sems.at[slot]
        )

    steps = total // STAGE
    for step in range(steps):
        slot = step % 2
        if step >= 2:
            copy_out(step - 2, slot).wait()
        part = acc[step * STAGE : (step + 1) * STAGE]
        stage[slot, :, :, :HD] = (part[:, :, :HD] * FACTOR).astype(jnp.bfloat16)
        stage[slot, :, :, HD:] = part[:, :, HD:].astype(jnp.bfloat16)
        copy_out(step, slot).start()
    for step in range(max(0, steps - 2), steps):
        copy_out(step, step % 2).wait()


def attention(table, stats, pairs, kv, glob):
    count, tile, _ = pairs.shape
    total = kv.shape[0]
    vmem = pl.BlockSpec(memory_space=pltpu.VMEM)
    return pl.pallas_call(
        attention_kernel,
        in_specs=[pl.BlockSpec(memory_space=pltpu.SMEM), vmem, vmem, vmem, vmem],
        out_specs=[vmem, pl.BlockSpec(memory_space=pl.ANY), vmem],
        out_shape=[
            jax.ShapeDtypeStruct((count, tile, HD), jnp.bfloat16),
            jax.ShapeDtypeStruct((total, tile, 2 * HD), jnp.bfloat16),
            jax.ShapeDtypeStruct((G, 2 * HD), jnp.float32),
        ],
        scratch_shapes=[
            pltpu.VMEM((total, tile, 2 * HD), jnp.float32),
            pltpu.VMEM((2, STAGE, tile, 2 * HD), jnp.bfloat16),
            pltpu.SemaphoreType.DMA((2,)),
        ],
        compiler_params=pltpu.CompilerParams(vmem_limit_bytes=60 * 1024 * 1024),
        cost_estimate=pl.CostEstimate(
            flops=count * (W + R + 1) * 10 * tile * BLK * HD,
            bytes_accessed=(total * 8 + count * 6) * tile * HD,
            transcendentals=count * (W + R + 1) * tile * BLK,
        ),
    )(table, stats, pairs, kv, glob)


def exchange(array):
    return lax.all_to_all(array, "seq", split_axis=0, concat_axis=0, tiled=True)


def to_mate(array, step, share):
    size = lax.axis_size("seq")
    return lax.ppermute(
        array, "seq", [(i, i - i % share + (i + step) % share) for i in range(size)]
    )


def body(
    queries,
    keys,
    values,
    saved_output,
    grad_output,
    log_norm,
    global_keys,
    global_values,
    flow_links,
    glob_owner,
):
    size = lax.axis_size("seq")
    tokens, features = queries.shape
    heads = features // HD
    blocks = tokens // BLK
    share = size // heads
    part = tokens // share
    tile = min(BLK, part)
    sub = part // tile
    pieces = BLK // tile
    count = size * sub
    mine = lax.axis_index("seq") % share

    kv_own = exchange(pair_heads(keys, values, share))
    glob_pair = jnp.concatenate(
        [global_keys.reshape(G, heads, HD), global_values.reshape(G, heads, HD)], axis=2
    )
    glob_out = jnp.repeat(jnp.transpose(glob_pair, (1, 0, 2)), share, axis=0)
    glob_in = exchange(glob_out)
    product = grad_output.astype(jnp.float32) * saved_output.astype(jnp.float32)
    delta = jnp.sum(product.reshape(tokens, heads, HD), axis=2).T
    stats_out = jnp.stack(
        [log_norm.reshape(size, part), delta.reshape(size, part)], axis=1
    )
    stats_in = exchange(stats_out)
    pairs = exchange(pair_heads(queries, grad_output, share))

    owners = jnp.arange(size, dtype=jnp.int32)[:, None] == glob_owner[None, :]
    glob_now = jnp.sum(
        jnp.where(owners[:, :, None], glob_in.astype(jnp.float32), 0.0), axis=0
    ).astype(jnp.bfloat16)
    stats = jnp.transpose(stats_in.reshape(size, 2, sub, tile), (0, 2, 1, 3)).reshape(
        count, 2, tile
    )
    kv = jnp.concatenate(
        [kv_own] + [to_mate(kv_own, share - step, share) for step in range(1, share)], axis=0
    ).reshape(share * count, tile, 2 * HD)

    order = jnp.arange(count, dtype=jnp.int32)
    my_blocks = (order // sub) * blocks + (mine * sub + order % sub) // pieces
    near = my_blocks[:, None] + jnp.arange(-1, 2, dtype=jnp.int32)[None, :]
    wanted = jnp.concatenate(
        [(near + size * blocks) % (size * blocks), flow_links[my_blocks]], axis=1
    )
    within = (wanted % blocks)[:, :, None] * pieces + jnp.arange(pieces, dtype=jnp.int32)
    offset = (within // sub - mine + share) % share
    table = offset * count + (wanted // blocks)[:, :, None] * sub + within % sub

    dq, dkv, dglob = attention(
        table.reshape(-1).astype(jnp.int32),
        stats,
        pairs.reshape(count, tile, 2 * HD),
        kv,
        glob_now,
    )
    dq_back = exchange(dq.reshape(size, part, HD))
    dkv = dkv.reshape(share, size, part, 2 * HD)
    dkv_sum = dkv[0].astype(jnp.float32)
    for step in range(1, share):
        dkv_sum = dkv_sum + to_mate(dkv[step], step, share).astype(jnp.float32)
    dkv_back = exchange(dkv_sum.astype(jnp.bfloat16))
    glob_parts = lax.all_gather(dglob, "seq", axis=0, tiled=False)
    glob_sum = jnp.sum(glob_parts.reshape(heads, share, G, 2, HD), axis=1)
    glob_grads = jnp.transpose(glob_sum, (2, 1, 0, 3)).reshape(2, G, features).astype(jnp.bfloat16)

    (grad_queries,) = unpair_heads(dq_back, share)
    grad_keys, grad_values = unpair_heads(dkv_back, share)
    return (grad_queries, grad_keys, grad_values, glob_grads[0], glob_grads[1])


def solution(mesh):
    return jax.shard_map(
        body,
        mesh=mesh,
        in_specs=(
            P("seq", "tp"),
            P("seq", "tp"),
            P("seq", "tp"),
            P("seq", "tp"),
            P("seq", "tp"),
            P("tp", "seq"),
            P("seq", None, "tp"),
            P("seq", None, "tp"),
            P(),
            P(),
        ),
        out_specs=(P("seq", "tp"), P("seq", "tp"), P("seq", "tp"), P(None, "tp"), P(None, "tp")),
        check_vma=False,
    )
```

```python
import functools
import math

import jax
import jax.numpy as jnp
from jax import lax
from jax.experimental import pallas as pl
from jax.experimental.pallas import tpu as pltpu
from jax.sharding import PartitionSpec as P

HD = 128
BLK = 128
R = 3
G = 128
W = 3
FACTOR = HD ** (-0.5)
LOG2E = math.log2(math.e)
STAGE = 4


def pair_kernel(left_ref, right_ref, out_ref):
    heads = out_ref.shape[0]
    for head in range(heads):
        cols = slice(head * HD, (head + 1) * HD)
        out_ref[head, 0, :, :HD] = left_ref[:, cols]
        out_ref[head, 0, :, HD:] = right_ref[:, cols]


def pair_heads(left, right, share):
    tokens, features = left.shape
    heads = features // HD
    part = tokens // share
    rows = min(256, part)
    steps = part // rows
    out = pl.pallas_call(
        pair_kernel,
        grid=(share, steps),
        in_specs=[pl.BlockSpec((rows, features), lambda s, t: (s * steps + t, 0))] * 2,
        out_specs=pl.BlockSpec((heads, 1, rows, 2 * HD), lambda s, t: (0, s, t, 0)),
        out_shape=jax.ShapeDtypeStruct((heads, share, part, 2 * HD), left.dtype),
        cost_estimate=pl.CostEstimate(
            flops=0, bytes_accessed=4 * tokens * features * 2, transcendentals=0
        ),
    )(left, right)
    return out.reshape(heads * share, part, 2 * HD)


def unpair_kernel(in_ref, *out_refs):
    heads = in_ref.shape[0]
    for head in range(heads):
        cols = slice(head * HD, (head + 1) * HD)
        for which, out_ref in enumerate(out_refs):
            out_ref[:, cols] = in_ref[head, 0, :, which * HD : (which + 1) * HD]


def unpair_heads(mixed, share):
    parts, part, width = mixed.shape
    heads = parts // share
    count = width // HD
    rows = min(256, part)
    steps = part // rows
    shape = jax.ShapeDtypeStruct((share * part, heads * HD), mixed.dtype)
    return pl.pallas_call(
        unpair_kernel,
        grid=(share, steps),
        in_specs=[pl.BlockSpec((heads, 1, rows, width), lambda s, t: (0, s, t, 0))],
        out_specs=[pl.BlockSpec((rows, heads * HD), lambda s, t: (s * steps + t, 0))] * count,
        out_shape=[shape] * count,
        cost_estimate=pl.CostEstimate(
            flops=0, bytes_accessed=4 * parts * part * width, transcendentals=0
        ),
    )(mixed.reshape(heads, share, part, width))


def attention_kernel(
    table_ref, stats_ref, pair_ref, kv_ref, glob_ref, dq_ref, dkv_ref, dglob_ref, acc, stage, sems
):
    count, tile, _ = pair_ref.shape
    total = acc.shape[0]
    kinds = (W + R) * (BLK // tile)

    def clear(block, carry):
        acc[block] = jnp.zeros((tile, 2 * HD), jnp.float32)
        return carry

    lax.fori_loop(0, total, clear, 0)
    dglob_ref[...] = jnp.zeros_like(dglob_ref)
    zero = jnp.zeros((tile, HD), jnp.bfloat16)

    def one_block(block, carry):
        pair = pair_ref[block]
        mixed = jnp.concatenate(
            [
                jnp.concatenate([pair[:, :HD], zero], axis=1),
                jnp.concatenate([zero, pair[:, HD:]], axis=1),
            ],
            axis=0,
        )
        stats = stats_ref[block]
        norm = stats[0:1] * LOG2E
        delta = stats[1:2]
        places = [table_ref[block * kinds + kind] for kind in range(kinds)]
        rows = jnp.concatenate([kv_ref[place] for place in places] + [glob_ref[...]], axis=0)
        both = lax.dot_general(
            rows, mixed, (((1,), (1,)), ((), ())), preferred_element_type=jnp.float32
        )
        attend = jnp.exp2(both[:, :tile] * (FACTOR * LOG2E) - norm)
        grad_scores = attend * (both[:, tile:] - delta)
        attend_low = attend.astype(jnp.bfloat16)
        scores_low = grad_scores.astype(jnp.bfloat16)
        grad_kv = jnp.dot(
            jnp.concatenate([scores_low, attend_low], axis=1),
            mixed,
            preferred_element_type=jnp.float32,
        )
        for kind, place in enumerate(places):
            acc[place] += grad_kv[kind * tile : (kind + 1) * tile]
        dglob_ref[...] += grad_kv[kinds * tile :]
        grad_q = lax.dot_general(
            scores_low, rows[:, :HD], (((0,), (0,)), ((), ())), preferred_element_type=jnp.float32
        )
        dq_ref[block] = (grad_q * FACTOR).astype(jnp.bfloat16)
        return carry

    lax.fori_loop(0, count, one_block, 0)
    dglob_ref[:, :HD] = dglob_ref[:, :HD] * FACTOR

    def copy_out(step, slot):
        return pltpu.make_async_copy(
            stage.at[slot], dkv_ref.at[pl.ds(step * STAGE, STAGE)], sems.at[slot]
        )

    steps = total // STAGE
    for step in range(steps):
        slot = step % 2
        if step >= 2:
            copy_out(step - 2, slot).wait()
        part = acc[step * STAGE : (step + 1) * STAGE]
        stage[slot, :, :, :HD] = (part[:, :, :HD] * FACTOR).astype(jnp.bfloat16)
        stage[slot, :, :, HD:] = part[:, :, HD:].astype(jnp.bfloat16)
        copy_out(step, slot).start()
    for step in range(max(0, steps - 2), steps):
        copy_out(step, step % 2).wait()


def attention(table, stats, pairs, kv, glob):
    count, tile, _ = pairs.shape
    total = kv.shape[0]
    vmem = pl.BlockSpec(memory_space=pltpu.VMEM)
    return pl.pallas_call(
        attention_kernel,
        in_specs=[pl.BlockSpec(memory_space=pltpu.SMEM), vmem, vmem, vmem, vmem],
        out_specs=[vmem, pl.BlockSpec(memory_space=pl.ANY), vmem],
        out_shape=[
            jax.ShapeDtypeStruct((count, tile, HD), jnp.bfloat16),
            jax.ShapeDtypeStruct((total, tile, 2 * HD), jnp.bfloat16),
            jax.ShapeDtypeStruct((G, 2 * HD), jnp.float32),
        ],
        scratch_shapes=[
            pltpu.VMEM((total, tile, 2 * HD), jnp.float32),
            pltpu.VMEM((2, STAGE, tile, 2 * HD), jnp.bfloat16),
            pltpu.SemaphoreType.DMA((2,)),
        ],
        compiler_params=pltpu.CompilerParams(vmem_limit_bytes=60 * 1024 * 1024),
        cost_estimate=pl.CostEstimate(
            flops=count * (W + R + 1) * 10 * tile * BLK * HD,
            bytes_accessed=(total * 8 + count * 6) * tile * HD,
            transcendentals=count * (W + R + 1) * tile * BLK,
        ),
    )(table, stats, pairs, kv, glob)


def exchange(array):
    return lax.all_to_all(array, "seq", split_axis=0, concat_axis=0, tiled=True)


def to_mate(array, step, share):
    size = lax.axis_size("seq")
    return lax.ppermute(
        array, "seq", [(i, i - i % share + (i + step) % share) for i in range(size)]
    )


def body_shared(
    queries,
    keys,
    values,
    saved_output,
    grad_output,
    log_norm,
    global_keys,
    global_values,
    flow_links,
    glob_owner,
):
    size = lax.axis_size("seq")
    tokens, features = queries.shape
    heads = features // HD
    blocks = tokens // BLK
    share = size // heads
    part = tokens // share
    tile = min(BLK, part)
    sub = part // tile
    pieces = BLK // tile
    count = size * sub
    mine = lax.axis_index("seq") % share

    kv_own = exchange(pair_heads(keys, values, share))
    glob_pair = jnp.concatenate(
        [global_keys.reshape(G, heads, HD), global_values.reshape(G, heads, HD)], axis=2
    )
    glob_out = jnp.repeat(jnp.transpose(glob_pair, (1, 0, 2)), share, axis=0)
    glob_in = exchange(glob_out)
    product = grad_output.astype(jnp.float32) * saved_output.astype(jnp.float32)
    delta = jnp.sum(product.reshape(tokens, heads, HD), axis=2).T
    stats_out = jnp.stack(
        [log_norm.reshape(size, part), delta.reshape(size, part)], axis=1
    )
    stats_in = exchange(stats_out)
    pairs = exchange(pair_heads(queries, grad_output, share))

    owners = jnp.arange(size, dtype=jnp.int32)[:, None] == glob_owner[None, :]
    glob_now = jnp.sum(
        jnp.where(owners[:, :, None], glob_in.astype(jnp.float32), 0.0), axis=0
    ).astype(jnp.bfloat16)
    stats = jnp.transpose(stats_in.reshape(size, 2, sub, tile), (0, 2, 1, 3)).reshape(
        count, 2, tile
    )
    kv = jnp.concatenate(
        [kv_own] + [to_mate(kv_own, share - step, share) for step in range(1, share)], axis=0
    ).reshape(share * count, tile, 2 * HD)

    order = jnp.arange(count, dtype=jnp.int32)
    my_blocks = (order // sub) * blocks + (mine * sub + order % sub) // pieces
    near = my_blocks[:, None] + jnp.arange(-1, 2, dtype=jnp.int32)[None, :]
    wanted = jnp.concatenate(
        [(near + size * blocks) % (size * blocks), flow_links[my_blocks]], axis=1
    )
    within = (wanted % blocks)[:, :, None] * pieces + jnp.arange(pieces, dtype=jnp.int32)
    offset = (within // sub - mine + share) % share
    table = offset * count + (wanted // blocks)[:, :, None] * sub + within % sub

    dq, dkv, dglob = attention(
        table.reshape(-1).astype(jnp.int32),
        stats,
        pairs.reshape(count, tile, 2 * HD),
        kv,
        glob_now,
    )
    dq_back = exchange(dq.reshape(size, part, HD))
    dkv = dkv.reshape(share, size, part, 2 * HD)
    dkv_sum = dkv[0].astype(jnp.float32)
    for step in range(1, share):
        dkv_sum = dkv_sum + to_mate(dkv[step], step, share).astype(jnp.float32)
    dkv_back = exchange(dkv_sum.astype(jnp.bfloat16))
    glob_parts = lax.all_gather(dglob, "seq", axis=0, tiled=False)
    glob_sum = jnp.sum(glob_parts.reshape(heads, share, G, 2, HD), axis=1)
    glob_grads = jnp.transpose(glob_sum, (2, 1, 0, 3)).reshape(2, G, features).astype(jnp.bfloat16)

    (grad_queries,) = unpair_heads(dq_back, share)
    grad_keys, grad_values = unpair_heads(dkv_back, share)
    return (grad_queries, grad_keys, grad_values, glob_grads[0], glob_grads[1])


CHUNKS = ((0, 1), (4, 4), (2, 2), (1, 1))
PAD = 8
VMEM_LIMIT = 60 * 1024 * 1024


def split_two(row):
    high = row.astype(jnp.bfloat16).astype(jnp.float32)
    return jnp.concatenate([high, row - high], axis=1)


def pack_queries_kernel(query_ref, grad_ref, saved_ref, norm_ref, out_ref):
    rows = query_ref.shape[0]
    for head in range(out_ref.shape[0]):
        cols = slice(head * HD, (head + 1) * HD)
        grad = grad_ref[:, cols]
        out_ref[head, :rows, :HD] = query_ref[:, cols]
        out_ref[head, :rows, HD:] = grad
        product = grad.astype(jnp.float32) * saved_ref[:, cols].astype(jnp.float32)
        delta = jnp.sum(product.T, axis=0, keepdims=True)
        norm = norm_ref[head : head + 1, :]
        stats = []
        for block in range(rows // BLK):
            lanes = slice(block * BLK, (block + 1) * BLK)
            stats += [split_two(norm[:, lanes]), split_two(delta[:, lanes])]
        if len(stats) < PAD:
            stats.append(jnp.zeros((PAD - len(stats), 2 * HD), jnp.float32))
        out_ref[head, rows:, :] = jnp.concatenate(stats, axis=0).astype(jnp.bfloat16)


def pack_queries(queries, grad_output, saved_output, log_norm, first, blocks):
    features = queries.shape[1]
    heads = features // HD
    rows = blocks * BLK
    spec = pl.BlockSpec((rows, features), lambda i: (first // blocks, 0))
    shape = (heads, rows + PAD, 2 * HD)
    return pl.pallas_call(
        pack_queries_kernel,
        grid=(1,),
        in_specs=[spec] * 3 + [pl.BlockSpec((heads, rows), lambda i: (0, first // blocks))],
        out_specs=pl.BlockSpec(shape, lambda i: (0, 0, 0)),
        out_shape=jax.ShapeDtypeStruct(shape, jnp.bfloat16),
        compiler_params=pltpu.CompilerParams(vmem_limit_bytes=VMEM_LIMIT),
        cost_estimate=pl.CostEstimate(
            flops=0, bytes_accessed=rows * features * 10, transcendentals=0
        ),
    )(queries, grad_output, saved_output, log_norm)


def pack_keys_kernel(key_ref, value_ref, glob_key_ref, glob_value_ref, out_ref):
    rows = key_ref.shape[0]
    for head in range(out_ref.shape[0]):
        cols = slice(head * HD, (head + 1) * HD)
        out_ref[head, :rows, :HD] = key_ref[:, cols]
        out_ref[head, :rows, HD:] = value_ref[:, cols]
        out_ref[head, rows:, :HD] = glob_key_ref[:, cols]
        out_ref[head, rows:, HD:] = glob_value_ref[:, cols]


def pack_keys(keys, values, glob_keys, glob_values):
    tokens, features = keys.shape
    heads = features // HD
    vmem = pl.BlockSpec(memory_space=pltpu.VMEM)
    return pl.pallas_call(
        pack_keys_kernel,
        in_specs=[vmem] * 4,
        out_specs=vmem,
        out_shape=jax.ShapeDtypeStruct((heads, tokens + G, 2 * HD), jnp.bfloat16),
        compiler_params=pltpu.CompilerParams(vmem_limit_bytes=VMEM_LIMIT),
        cost_estimate=pl.CostEstimate(
            flops=0, bytes_accessed=(tokens + G) * features * 8, transcendentals=0
        ),
    )(keys, values, glob_keys, glob_values)


def pair_grads(pair, stats, rows, valid):
    zero = jnp.zeros((BLK, HD), jnp.bfloat16)
    mixed = jnp.concatenate(
        [
            jnp.concatenate([pair[:, :HD], zero], axis=1),
            jnp.concatenate([zero, pair[:, HD:]], axis=1),
        ],
        axis=0,
    )
    norm = (stats[0:1, :HD] + stats[0:1, HD:]) * LOG2E
    delta = stats[1:2, :HD] + stats[1:2, HD:]
    rows = jnp.concatenate(rows, axis=0) if len(rows) > 1 else rows[0]
    both = lax.dot_general(
        rows, mixed, (((1,), (1,)), ((), ())), preferred_element_type=jnp.float32
    )
    attend = jnp.exp2(both[:, :HD] * (FACTOR * LOG2E) - norm)
    parts = []
    for kind, known in enumerate(valid):
        part = attend[kind * BLK : (kind + 1) * BLK]
        parts.append(part if known is None else jnp.where(known, part, 0.0))
    attend = jnp.concatenate(parts, axis=0) if len(parts) > 1 else parts[0]
    grad_scores = attend * (both[:, HD:] - delta)
    scores_low = grad_scores.astype(jnp.bfloat16)
    grad_kv = jnp.dot(
        jnp.concatenate([scores_low, attend.astype(jnp.bfloat16)], axis=1),
        mixed,
        preferred_element_type=jnp.float32,
    )
    grad_q = lax.dot_general(
        scores_low, rows[:, :HD], (((0,), (0,)), ((), ())), preferred_element_type=jnp.float32
    )
    return grad_kv, grad_q * FACTOR


def key_rows(kv_ref, place, blocks):
    source = place // blocks
    start = pl.multiple_of((place % blocks) * BLK, BLK)
    return kv_ref[source, pl.ds(start, BLK), :]


def own_kernel(table_ref, *refs):
    chunk_refs, (kv_ref, glob_ref) = refs[: len(CHUNKS)], refs[len(CHUNKS) : len(CHUNKS) + 2]
    dq_refs, (dkv_ref, dglob_ref) = refs[len(CHUNKS) + 2 : -2], refs[-2:]
    sources = kv_ref.shape[0]
    blocks = dkv_ref.shape[0] // sources
    kinds = W + R

    def clear(block, carry):
        dkv_ref[block] = jnp.zeros((BLK, 2 * HD), jnp.float32)
        return carry

    lax.fori_loop(0, dkv_ref.shape[0], clear, 0)
    dglob_ref[...] = jnp.zeros_like(dglob_ref)
    for (first, size), pair_ref, dq_ref in zip(CHUNKS, chunk_refs, dq_refs):

        def one_source(source, carry, first=first, size=size, pair_ref=pair_ref, dq_ref=dq_ref):
            stats = pair_ref[source, size * BLK :, :].astype(jnp.float32)
            for inner in range(size):
                lines = slice(inner * BLK, (inner + 1) * BLK)
                entry = (source * blocks + first + inner) * kinds
                wanted = [table_ref[entry + kind] for kind in range(kinds)]
                places = [jnp.maximum(place, 0) for place in wanted]
                rows = [key_rows(kv_ref, place, blocks) for place in places]
                grad_kv, grad_q = pair_grads(
                    pair_ref[source, lines, :],
                    stats[2 * inner : 2 * inner + 2],
                    rows + [glob_ref[...]],
                    [place >= 0 for place in wanted] + [None],
                )
                for kind, place in enumerate(places):
                    dkv_ref[place] += grad_kv[kind * BLK : (kind + 1) * BLK]
                dglob_ref[...] += grad_kv[kinds * BLK :]
                dq_ref[source, lines, :] = grad_q
            return carry

        lax.fori_loop(0, sources, one_source, 0)
    dglob_ref[:, :HD] = dglob_ref[:, :HD] * FACTOR


def own_pairs(table, chunks, kv, glob):
    sources = kv.shape[0]
    blocks = (kv.shape[1] - G) // BLK
    vmem = pl.BlockSpec(memory_space=pltpu.VMEM)
    smem = pl.BlockSpec(memory_space=pltpu.SMEM)
    units = sources * blocks * (W + R + 1)
    return pl.pallas_call(
        own_kernel,
        in_specs=[smem] + [vmem] * (len(chunks) + 2),
        out_specs=[vmem] * (len(chunks) + 2),
        out_shape=[
            jax.ShapeDtypeStruct((sources, size * BLK, HD), jnp.float32) for _, size in CHUNKS
        ]
        + [
            jax.ShapeDtypeStruct((sources * blocks, BLK, 2 * HD), jnp.float32),
            jax.ShapeDtypeStruct((G, 2 * HD), jnp.float32),
        ],
        compiler_params=pltpu.CompilerParams(vmem_limit_bytes=VMEM_LIMIT),
        cost_estimate=pl.CostEstimate(flops=0, bytes_accessed=1024, transcendentals=0),
    )(table, *chunks, kv, glob)


def cross_kernel(first, size, last, table_ref, pair_ref, kv_ref, sum_ref, dq_ref, dkv_ref):
    sources = kv_ref.shape[0]
    total = sum_ref.shape[0]
    blocks = total // sources

    def one_source(source, carry):
        stats = pair_ref[source, size * BLK :, :].astype(jnp.float32)
        for inner in range(size):
            lines = slice(inner * BLK, (inner + 1) * BLK)
            entry = (source * blocks + first + inner) * R
            wanted = [table_ref[entry + kind] for kind in range(R)]
            places = [jnp.maximum(place, 0) for place in wanted]
            grad_kv, grad_q = pair_grads(
                pair_ref[source, lines, :],
                stats[2 * inner : 2 * inner + 2],
                [key_rows(kv_ref, place, blocks) for place in places],
                [place >= 0 for place in wanted],
            )
            for kind, place in enumerate(places):
                sum_ref[place] += grad_kv[kind * BLK : (kind + 1) * BLK]
            dq_ref[source, lines, :] = grad_q.astype(jnp.bfloat16)
        return carry

    lax.fori_loop(0, sources, one_source, 0)
    rims = []
    if first == 0:
        rims.append((0, 0, total - 1))
    if first + size == blocks:
        rims.append((sources - 1, size - 1, 0))
    for source, inner, place in rims:
        lines = slice(inner * BLK, (inner + 1) * BLK)
        stats = pair_ref[source, size * BLK :, :].astype(jnp.float32)
        grad_kv, grad_q = pair_grads(
            pair_ref[source, lines, :],
            stats[2 * inner : 2 * inner + 2],
            [key_rows(kv_ref, place, blocks)],
            [None],
        )
        sum_ref[place] += grad_kv
        dq_ref[source, lines, :] = (
            dq_ref[source, lines, :].astype(jnp.float32) + grad_q
        ).astype(jnp.bfloat16)
    if last:

        def round_block(block, carry):
            start = pl.multiple_of((block % blocks) * BLK, BLK)
            value = sum_ref[block]
            dkv_ref[block // blocks, pl.ds(start, BLK), :] = jnp.concatenate(
                [value[:, :HD] * FACTOR, value[:, HD:]], axis=1
            ).astype(jnp.bfloat16)
            return carry

        lax.fori_loop(0, total, round_block, 0)


def cross_middle_kernel(first, size, table_ref, pair_ref, kv_ref, in_ref, dq_ref, sum_ref):
    def carry_over(block, carry):
        sum_ref[block] = in_ref[block]
        return carry

    lax.fori_loop(0, sum_ref.shape[0], carry_over, 0)
    cross_kernel(first, size, False, table_ref, pair_ref, kv_ref, sum_ref, dq_ref, None)


def cross_last_kernel(first, size, table_ref, pair_ref, kv_ref, in_ref, dq_ref, dkv_ref, sum_ref):
    def carry_over(block, carry):
        sum_ref[block] = in_ref[block]
        return carry

    lax.fori_loop(0, sum_ref.shape[0], carry_over, 0)
    cross_kernel(first, size, True, table_ref, pair_ref, kv_ref, sum_ref, dq_ref, dkv_ref)


def cross_pairs(table, pairs, kv, sums, first, size, last):
    sources = kv.shape[0]
    blocks = (kv.shape[1] - G) // BLK
    vmem = pl.BlockSpec(memory_space=pltpu.VMEM)
    smem = pl.BlockSpec(memory_space=pltpu.SMEM)
    units = sources * size * R
    dq_shape = jax.ShapeDtypeStruct((sources, size * BLK, HD), jnp.bfloat16)
    if last:
        kernel = functools.partial(cross_last_kernel, first, size)
        sum_shape = jax.ShapeDtypeStruct((sources, blocks * BLK, 2 * HD), jnp.bfloat16)
        scratch = [pltpu.VMEM(sums.shape, jnp.float32)]
    else:
        kernel = functools.partial(cross_middle_kernel, first, size)
        sum_shape = jax.ShapeDtypeStruct(sums.shape, jnp.float32)
        scratch = []
    return pl.pallas_call(
        kernel,
        in_specs=[smem, vmem, vmem, vmem],
        out_specs=[vmem, vmem],
        out_shape=[dq_shape, sum_shape],
        scratch_shapes=scratch,
        compiler_params=pltpu.CompilerParams(vmem_limit_bytes=VMEM_LIMIT),
        cost_estimate=pl.CostEstimate(flops=0, bytes_accessed=1024, transcendentals=0),
    )(table, pairs, kv, sums)


def unpack_kernel(groups, *refs):
    in_refs, out_ref = refs[:-1], refs[-1]
    for in_ref, places in zip(in_refs, groups):
        start = 0
        for first, size in places:
            for head in range(in_ref.shape[0]):
                out_ref[first * BLK : (first + size) * BLK, head * HD : (head + 1) * HD] = in_ref[
                    head, start : start + size * BLK, :
                ]
            start += size * BLK


def unpack_queries(arrays, groups):
    heads = arrays[0].shape[0]
    tokens = sum(array.shape[1] for array in arrays)
    vmem = pl.BlockSpec(memory_space=pltpu.VMEM)
    return pl.pallas_call(
        functools.partial(unpack_kernel, groups),
        in_specs=[vmem] * len(arrays),
        out_specs=vmem,
        out_shape=jax.ShapeDtypeStruct((tokens, heads * HD), jnp.bfloat16),
        compiler_params=pltpu.CompilerParams(vmem_limit_bytes=VMEM_LIMIT),
        cost_estimate=pl.CostEstimate(
            flops=0, bytes_accessed=tokens * heads * HD * 4, transcendentals=0
        ),
    )(*arrays)


def body_halves(
    queries,
    keys,
    values,
    saved_output,
    grad_output,
    log_norm,
    global_keys,
    global_values,
    flow_links,
    glob_owner,
):
    size = lax.axis_size("seq")
    my_index = lax.axis_index("seq")
    tokens, features = queries.shape
    heads = features // HD
    blocks = tokens // BLK
    count = heads * blocks
    half = my_index // heads
    groups = [list(range(heads)), list(range(heads, size))]

    def within(array):
        return lax.all_to_all(
            array, "seq", split_axis=0, concat_axis=0, tiled=True, axis_index_groups=groups
        )

    def across(array):
        return lax.ppermute(array, "seq", [(i, (i + heads) % size) for i in range(size)])

    chunks, crossed = [], []
    for first, number in CHUNKS:
        packed = pack_queries(queries, grad_output, saved_output, log_norm, first, number)
        if chunks:
            packed, chunks[-1] = lax.optimization_barrier((packed, chunks[-1]))
        chunk = within(packed)
        chunks.append(chunk)
        crossed.append(across(chunk))
    owned = (glob_owner == my_index)[:, None]
    packed = pack_keys(
        keys,
        values,
        jnp.where(owned, global_keys[0], jnp.bfloat16(0)),
        jnp.where(owned, global_values[0], jnp.bfloat16(0)),
    )
    packed, chunks[-1] = lax.optimization_barrier((packed, chunks[-1]))
    kv = within(packed)
    glob_half = jnp.sum(kv[:, tokens:, :].astype(jnp.float32), axis=0).astype(jnp.bfloat16)
    glob_now = (glob_half.astype(jnp.float32) + across(glob_half).astype(jnp.float32)).astype(
        jnp.bfloat16
    )

    def places(wanted):
        here = wanted - half * count
        return jnp.where((here >= 0) & (here < count), here, -1).reshape(-1).astype(jnp.int32)

    links = flow_links.reshape(2, count, R)
    my_links = lax.dynamic_index_in_dim(links, half, axis=0, keepdims=False)
    other_links = lax.dynamic_index_in_dim(links, 1 - half, axis=0, keepdims=False)
    mine = half * count + jnp.arange(count, dtype=jnp.int32)
    near = (mine[:, None] + jnp.arange(-1, 2, dtype=jnp.int32) + 2 * count) % (2 * count)
    own_table = places(jnp.concatenate([near, my_links], axis=1))
    cross_table = places(other_links)

    *own_dq, sums, dglob = own_pairs(own_table, chunks, kv, glob_now)
    glob_parts = lax.all_gather(dglob, "seq", axis=0, tiled=False)
    totals = []
    for step, (first, number) in enumerate(CHUNKS):
        dq, sums = cross_pairs(
            cross_table, crossed[step], kv, sums, first, number, step == len(CHUNKS) - 1
        )
        totals.append(
            (own_dq[step] + across(dq).astype(jnp.float32)).astype(jnp.bfloat16)
        )
    sums = within(sums)
    totals[-1], sums = lax.optimization_barrier((totals[-1], sums))
    grad_keys, grad_values = unpair_heads(sums, 1)
    early = within(jnp.concatenate(totals[:-1], axis=1))
    late = within(totals[-1])
    grad_queries = unpack_queries((early, late), (CHUNKS[:-1], CHUNKS[-1:]))
    glob_sum = jnp.sum(glob_parts.reshape(2, heads, G, 2, HD), axis=0)
    glob_grads = jnp.transpose(glob_sum, (2, 1, 0, 3)).reshape(2, G, features).astype(jnp.bfloat16)
    return (grad_queries, grad_keys, grad_values, glob_grads[0], glob_grads[1])


def body(queries, *rest):
    heads = queries.shape[1] // HD
    blocks = queries.shape[0] // BLK
    if lax.axis_size("seq") == 2 * heads and blocks == sum(number for _, number in CHUNKS):
        return body_halves(queries, *rest)
    return body_shared(queries, *rest)


def solution(mesh):
    return jax.shard_map(
        body,
        mesh=mesh,
        in_specs=(
            P("seq", "tp"),
            P("seq", "tp"),
            P("seq", "tp"),
            P("seq", "tp"),
            P("seq", "tp"),
            P("tp", "seq"),
            P("seq", None, "tp"),
            P("seq", None, "tp"),
            P(),
            P(),
        ),
        out_specs=(P("seq", "tp"), P("seq", "tp"), P("seq", "tp"), P(None, "tp"), P(None, "tp")),
        check_vma=False,
    )
```

```python
import functools
import math

import jax
import jax.numpy as jnp
from jax import lax
from jax.experimental import pallas as pl
from jax.experimental.pallas import tpu as pltpu
from jax.sharding import PartitionSpec as P

HD = 128
BLK = 128
R = 3
G = 128
W = 3
FACTOR = HD ** (-0.5)
LOG2E = math.log2(math.e)
STAGE = 4


def pair_kernel(left_ref, right_ref, out_ref):
    heads = out_ref.shape[0]
    for head in range(heads):
        cols = slice(head * HD, (head + 1) * HD)
        out_ref[head, 0, :, :HD] = left_ref[:, cols]
        out_ref[head, 0, :, HD:] = right_ref[:, cols]


def pair_heads(left, right, share):
    tokens, features = left.shape
    heads = features // HD
    part = tokens // share
    rows = min(256, part)
    steps = part // rows
    out = pl.pallas_call(
        pair_kernel,
        grid=(share, steps),
        in_specs=[pl.BlockSpec((rows, features), lambda s, t: (s * steps + t, 0))] * 2,
        out_specs=pl.BlockSpec((heads, 1, rows, 2 * HD), lambda s, t: (0, s, t, 0)),
        out_shape=jax.ShapeDtypeStruct((heads, share, part, 2 * HD), left.dtype),
        cost_estimate=pl.CostEstimate(
            flops=0, bytes_accessed=4 * tokens * features * 2, transcendentals=0
        ),
    )(left, right)
    return out.reshape(heads * share, part, 2 * HD)


def unpair_kernel(in_ref, *out_refs):
    heads = in_ref.shape[0]
    for head in range(heads):
        cols = slice(head * HD, (head + 1) * HD)
        for which, out_ref in enumerate(out_refs):
            out_ref[:, cols] = in_ref[head, 0, :, which * HD : (which + 1) * HD]


def unpair_heads(mixed, share):
    parts, part, width = mixed.shape
    heads = parts // share
    count = width // HD
    rows = min(256, part)
    steps = part // rows
    shape = jax.ShapeDtypeStruct((share * part, heads * HD), mixed.dtype)
    return pl.pallas_call(
        unpair_kernel,
        grid=(share, steps),
        in_specs=[pl.BlockSpec((heads, 1, rows, width), lambda s, t: (0, s, t, 0))],
        out_specs=[pl.BlockSpec((rows, heads * HD), lambda s, t: (s * steps + t, 0))] * count,
        out_shape=[shape] * count,
        cost_estimate=pl.CostEstimate(
            flops=0, bytes_accessed=4 * parts * part * width, transcendentals=0
        ),
    )(mixed.reshape(heads, share, part, width))


def attention_kernel(
    table_ref, stats_ref, pair_ref, kv_ref, glob_ref, dq_ref, dkv_ref, dglob_ref, acc, stage, sems
):
    count, tile, _ = pair_ref.shape
    total = acc.shape[0]
    kinds = (W + R) * (BLK // tile)

    def clear(block, carry):
        acc[block] = jnp.zeros((tile, 2 * HD), jnp.float32)
        return carry

    lax.fori_loop(0, total, clear, 0)
    dglob_ref[...] = jnp.zeros_like(dglob_ref)
    zero = jnp.zeros((tile, HD), jnp.bfloat16)

    def one_block(block, carry):
        pair = pair_ref[block]
        mixed = jnp.concatenate(
            [
                jnp.concatenate([pair[:, :HD], zero], axis=1),
                jnp.concatenate([zero, pair[:, HD:]], axis=1),
            ],
            axis=0,
        )
        stats = stats_ref[block]
        norm = stats[0:1] * LOG2E
        delta = stats[1:2]
        places = [table_ref[block * kinds + kind] for kind in range(kinds)]
        rows = jnp.concatenate([kv_ref[place] for place in places] + [glob_ref[...]], axis=0)
        both = lax.dot_general(
            rows, mixed, (((1,), (1,)), ((), ())), preferred_element_type=jnp.float32
        )
        attend = jnp.exp2(both[:, :tile] * (FACTOR * LOG2E) - norm)
        grad_scores = attend * (both[:, tile:] - delta)
        attend_low = attend.astype(jnp.bfloat16)
        scores_low = grad_scores.astype(jnp.bfloat16)
        grad_kv = jnp.dot(
            jnp.concatenate([scores_low, attend_low], axis=1),
            mixed,
            preferred_element_type=jnp.float32,
        )
        for kind, place in enumerate(places):
            acc[place] += grad_kv[kind * tile : (kind + 1) * tile]
        dglob_ref[...] += grad_kv[kinds * tile :]
        grad_q = lax.dot_general(
            scores_low, rows[:, :HD], (((0,), (0,)), ((), ())), preferred_element_type=jnp.float32
        )
        dq_ref[block] = (grad_q * FACTOR).astype(jnp.bfloat16)
        return carry

    lax.fori_loop(0, count, one_block, 0)
    dglob_ref[:, :HD] = dglob_ref[:, :HD] * FACTOR

    def copy_out(step, slot):
        return pltpu.make_async_copy(
            stage.at[slot], dkv_ref.at[pl.ds(step * STAGE, STAGE)], sems.at[slot]
        )

    steps = total // STAGE
    for step in range(steps):
        slot = step % 2
        if step >= 2:
            copy_out(step - 2, slot).wait()
        part = acc[step * STAGE : (step + 1) * STAGE]
        stage[slot, :, :, :HD] = (part[:, :, :HD] * FACTOR).astype(jnp.bfloat16)
        stage[slot, :, :, HD:] = part[:, :, HD:].astype(jnp.bfloat16)
        copy_out(step, slot).start()
    for step in range(max(0, steps - 2), steps):
        copy_out(step, step % 2).wait()


def attention(table, stats, pairs, kv, glob):
    count, tile, _ = pairs.shape
    total = kv.shape[0]
    vmem = pl.BlockSpec(memory_space=pltpu.VMEM)
    return pl.pallas_call(
        attention_kernel,
        in_specs=[pl.BlockSpec(memory_space=pltpu.SMEM), vmem, vmem, vmem, vmem],
        out_specs=[vmem, pl.BlockSpec(memory_space=pl.ANY), vmem],
        out_shape=[
            jax.ShapeDtypeStruct((count, tile, HD), jnp.bfloat16),
            jax.ShapeDtypeStruct((total, tile, 2 * HD), jnp.bfloat16),
            jax.ShapeDtypeStruct((G, 2 * HD), jnp.float32),
        ],
        scratch_shapes=[
            pltpu.VMEM((total, tile, 2 * HD), jnp.float32),
            pltpu.VMEM((2, STAGE, tile, 2 * HD), jnp.bfloat16),
            pltpu.SemaphoreType.DMA((2,)),
        ],
        compiler_params=pltpu.CompilerParams(vmem_limit_bytes=60 * 1024 * 1024),
        cost_estimate=pl.CostEstimate(
            flops=count * (W + R + 1) * 10 * tile * BLK * HD,
            bytes_accessed=(total * 8 + count * 6) * tile * HD,
            transcendentals=count * (W + R + 1) * tile * BLK,
        ),
    )(table, stats, pairs, kv, glob)


def exchange(array):
    return lax.all_to_all(array, "seq", split_axis=0, concat_axis=0, tiled=True)


def to_mate(array, step, share):
    size = lax.axis_size("seq")
    return lax.ppermute(
        array, "seq", [(i, i - i % share + (i + step) % share) for i in range(size)]
    )


def body_shared(
    queries,
    keys,
    values,
    saved_output,
    grad_output,
    log_norm,
    global_keys,
    global_values,
    flow_links,
    glob_owner,
):
    size = lax.axis_size("seq")
    tokens, features = queries.shape
    heads = features // HD
    blocks = tokens // BLK
    share = size // heads
    part = tokens // share
    tile = min(BLK, part)
    sub = part // tile
    pieces = BLK // tile
    count = size * sub
    mine = lax.axis_index("seq") % share

    kv_own = exchange(pair_heads(keys, values, share))
    glob_pair = jnp.concatenate(
        [global_keys.reshape(G, heads, HD), global_values.reshape(G, heads, HD)], axis=2
    )
    glob_out = jnp.repeat(jnp.transpose(glob_pair, (1, 0, 2)), share, axis=0)
    glob_in = exchange(glob_out)
    product = grad_output.astype(jnp.float32) * saved_output.astype(jnp.float32)
    delta = jnp.sum(product.reshape(tokens, heads, HD), axis=2).T
    stats_out = jnp.stack(
        [log_norm.reshape(size, part), delta.reshape(size, part)], axis=1
    )
    stats_in = exchange(stats_out)
    pairs = exchange(pair_heads(queries, grad_output, share))

    owners = jnp.arange(size, dtype=jnp.int32)[:, None] == glob_owner[None, :]
    glob_now = jnp.sum(
        jnp.where(owners[:, :, None], glob_in.astype(jnp.float32), 0.0), axis=0
    ).astype(jnp.bfloat16)
    stats = jnp.transpose(stats_in.reshape(size, 2, sub, tile), (0, 2, 1, 3)).reshape(
        count, 2, tile
    )
    kv = jnp.concatenate(
        [kv_own] + [to_mate(kv_own, share - step, share) for step in range(1, share)], axis=0
    ).reshape(share * count, tile, 2 * HD)

    order = jnp.arange(count, dtype=jnp.int32)
    my_blocks = (order // sub) * blocks + (mine * sub + order % sub) // pieces
    near = my_blocks[:, None] + jnp.arange(-1, 2, dtype=jnp.int32)[None, :]
    wanted = jnp.concatenate(
        [(near + size * blocks) % (size * blocks), flow_links[my_blocks]], axis=1
    )
    within = (wanted % blocks)[:, :, None] * pieces + jnp.arange(pieces, dtype=jnp.int32)
    offset = (within // sub - mine + share) % share
    table = offset * count + (wanted // blocks)[:, :, None] * sub + within % sub

    dq, dkv, dglob = attention(
        table.reshape(-1).astype(jnp.int32),
        stats,
        pairs.reshape(count, tile, 2 * HD),
        kv,
        glob_now,
    )
    dq_back = exchange(dq.reshape(size, part, HD))
    dkv = dkv.reshape(share, size, part, 2 * HD)
    dkv_sum = dkv[0].astype(jnp.float32)
    for step in range(1, share):
        dkv_sum = dkv_sum + to_mate(dkv[step], step, share).astype(jnp.float32)
    dkv_back = exchange(dkv_sum.astype(jnp.bfloat16))
    glob_parts = lax.all_gather(dglob, "seq", axis=0, tiled=False)
    glob_sum = jnp.sum(glob_parts.reshape(heads, share, G, 2, HD), axis=1)
    glob_grads = jnp.transpose(glob_sum, (2, 1, 0, 3)).reshape(2, G, features).astype(jnp.bfloat16)

    (grad_queries,) = unpair_heads(dq_back, share)
    grad_keys, grad_values = unpair_heads(dkv_back, share)
    return (grad_queries, grad_keys, grad_values, glob_grads[0], glob_grads[1])


PAD = 8
CHUNKS = 2
VMEM_LIMIT = 60 * 1024 * 1024


def split_two(row):
    high = row.astype(jnp.bfloat16).astype(jnp.float32)
    return jnp.concatenate([high, row - high], axis=1)


def pack_kernel(query_ref, grad_ref, saved_ref, norm_ref, *refs):
    *kv_refs, out_ref = refs
    rows = query_ref.shape[0]
    base = out_ref.shape[2] - rows - PAD
    for head in range(out_ref.shape[0]):
        cols = slice(head * HD, (head + 1) * HD)
        for which, kv_ref in enumerate(kv_refs):
            out_ref[head, 0, :base, which * HD : (which + 1) * HD] = kv_ref[:, cols]
        grad = grad_ref[:, cols]
        out_ref[head, 0, base : base + rows, :HD] = query_ref[:, cols]
        out_ref[head, 0, base : base + rows, HD:] = grad
        product = grad.astype(jnp.float32) * saved_ref[:, cols].astype(jnp.float32)
        delta = jnp.sum(product.T, axis=0, keepdims=True)
        norm = norm_ref[head : head + 1, :]
        stats = []
        for block in range(rows // BLK):
            lanes = slice(block * BLK, (block + 1) * BLK)
            stats += [split_two(norm[:, lanes]), split_two(delta[:, lanes])]
        stats.append(jnp.zeros((PAD - len(stats), 2 * HD), jnp.float32))
        out_ref[head, 0, base + rows :, :] = jnp.concatenate(stats, axis=0).astype(jnp.bfloat16)


def pack(queries, grad_output, saved_output, log_norm, chunk, share, *kv):
    tokens, features = queries.shape
    heads = features // HD
    part = tokens // share
    rows = part // CHUNKS
    base = part if kv else 0
    height = base + rows + PAD
    spec = pl.BlockSpec((rows, features), lambda s: (s * CHUNKS + chunk, 0))
    out = pl.pallas_call(
        pack_kernel,
        grid=(share,),
        in_specs=[spec] * 3
        + [pl.BlockSpec((heads, rows), lambda s: (0, s * CHUNKS + chunk))]
        + [pl.BlockSpec((part, features), lambda s: (s, 0))] * len(kv),
        out_specs=pl.BlockSpec((heads, 1, height, 2 * HD), lambda s: (0, s, 0, 0)),
        out_shape=jax.ShapeDtypeStruct((heads, share, height, 2 * HD), jnp.bfloat16),
        compiler_params=pltpu.CompilerParams(vmem_limit_bytes=VMEM_LIMIT),
        cost_estimate=pl.CostEstimate(
            flops=0, bytes_accessed=share * height * features * 8, transcendentals=0
        ),
    )(queries, grad_output, saved_output, log_norm, *kv)
    return out.reshape(heads * share, height, 2 * HD)


def pair_grads(pair, stats, rows):
    zero = jnp.zeros((BLK, HD), jnp.bfloat16)
    mixed = jnp.concatenate(
        [
            jnp.concatenate([pair[:, :HD], zero], axis=1),
            jnp.concatenate([zero, pair[:, HD:]], axis=1),
        ],
        axis=0,
    )
    norm = (stats[0:1, :HD] + stats[0:1, HD:]) * LOG2E
    delta = stats[1:2, :HD] + stats[1:2, HD:]
    rows = jnp.concatenate(rows, axis=0)
    both = lax.dot_general(
        rows, mixed, (((1,), (1,)), ((), ())), preferred_element_type=jnp.float32
    )
    attend = jnp.exp2(both[:, :HD] * (FACTOR * LOG2E) - norm)
    grad_scores = attend * (both[:, HD:] - delta)
    scores_low = grad_scores.astype(jnp.bfloat16)
    grad_kv = jnp.dot(
        jnp.concatenate([scores_low, attend.astype(jnp.bfloat16)], axis=1),
        mixed,
        preferred_element_type=jnp.float32,
    )
    grad_q = lax.dot_general(
        scores_low, rows[:, :HD], (((0,), (0,)), ((), ())), preferred_element_type=jnp.float32
    )
    return grad_kv, grad_q * FACTOR


def chunk_kernel(last, base, table_ref, glob_ref, own_ref, mate_ref, pair_ref, *refs):
    if last:
        before_ref, glob_before_ref, dq_ref, keep_ref, give_ref, dglob_ref = refs[:6]
        kv, pairs, acc, sems, before, stage, out_sems = refs[6:]
    else:
        dq_ref, sum_ref, dglob_ref, kv, pairs, acc, sems = refs
    sources = pairs.shape[0]
    blocks = (pairs.shape[1] - PAD) // BLK
    sub = kv.shape[1] // BLK
    total = acc.shape[0]
    kinds = W + R
    copies = [
        pltpu.make_async_copy(
            own_ref.at[:, pl.ds(0, sub * BLK), :], kv.at[pl.ds(0, sources)], sems.at[0]
        ),
        pltpu.make_async_copy(
            mate_ref.at[:, pl.ds(0, sub * BLK), :], kv.at[pl.ds(sources, sources)], sems.at[1]
        ),
        pltpu.make_async_copy(
            pair_ref.at[:, pl.ds(base, pairs.shape[1]), :], pairs, sems.at[2]
        ),
    ]
    for copy in copies:
        copy.start()
    if last:
        earlier = pltpu.make_async_copy(before_ref, before, sems.at[3])
        earlier.start()
        dglob_ref[...] = glob_before_ref[...]
    else:
        dglob_ref[...] = jnp.zeros_like(dglob_ref)

    def clear(block, carry):
        acc[block] = jnp.zeros((BLK, 2 * HD), jnp.float32)
        return carry

    lax.fori_loop(0, total, clear, 0)
    for copy in copies:
        copy.wait()

    def one_source(source, carry):
        stats = pairs[source, blocks * BLK :, :].astype(jnp.float32)
        for inner in range(blocks):
            lines = slice(inner * BLK, (inner + 1) * BLK)
            entry = (source * blocks + inner) * kinds
            places = [table_ref[entry + kind] for kind in range(kinds)]
            rows = [
                kv[place // sub, pl.ds(pl.multiple_of((place % sub) * BLK, BLK), BLK), :]
                for place in places
            ]
            grad_kv, grad_q = pair_grads(
                pairs[source, lines, :], stats[2 * inner : 2 * inner + 2], rows + [glob_ref[...]]
            )
            for kind, place in enumerate(places):
                acc[place] += grad_kv[kind * BLK : (kind + 1) * BLK]
            dglob_ref[...] += grad_kv[kinds * BLK :]
            dq_ref[source, lines, :] = grad_q.astype(jnp.bfloat16)
        return carry

    lax.fori_loop(0, sources, one_source, 0)
    if not last:
        leave = pltpu.make_async_copy(acc, sum_ref, sems.at[3])
        leave.start()
        leave.wait()
        return
    dglob_ref[:, :HD] = dglob_ref[:, :HD] * FACTOR
    earlier.wait()

    def copy_out(group):
        slot = group % 2
        out = keep_ref.at[group] if group < sources else give_ref.at[group - sources]
        return pltpu.make_async_copy(stage.at[slot], out, out_sems.at[slot])

    groups = total // sub
    for group in range(groups):
        if group >= 2:
            copy_out(group - 2).wait()
        for inner in range(sub):
            value = acc[group * sub + inner] + before[group * sub + inner]
            lines = slice(inner * BLK, (inner + 1) * BLK)
            stage[group % 2, lines, :HD] = (value[:, :HD] * FACTOR).astype(jnp.bfloat16)
            stage[group % 2, lines, HD:] = value[:, HD:].astype(jnp.bfloat16)
        copy_out(group).start()
    for group in range(max(0, groups - 2), groups):
        copy_out(group).wait()


def chunk_call(table, glob, own, mate, pairs, base, part, before=None):
    sources = own.shape[0]
    rows = pairs.shape[1] - base - PAD
    total = 2 * sources * (part // BLK)
    last = before is not None
    vmem = pl.BlockSpec(memory_space=pltpu.VMEM)
    smem = pl.BlockSpec(memory_space=pltpu.SMEM)
    hbm = pl.BlockSpec(memory_space=pl.ANY)
    sums = jax.ShapeDtypeStruct((total, BLK, 2 * HD), jnp.float32)
    rounded = jax.ShapeDtypeStruct((sources, part, 2 * HD), jnp.bfloat16)
    scratch = [
        pltpu.VMEM((2 * sources, part, 2 * HD), jnp.bfloat16),
        pltpu.VMEM((sources, rows + PAD, 2 * HD), jnp.bfloat16),
        pltpu.VMEM(sums.shape, jnp.float32),
        pltpu.SemaphoreType.DMA((4,)),
    ]
    if last:
        scratch += [
            pltpu.VMEM(sums.shape, jnp.float32),
            pltpu.VMEM((2, part, 2 * HD), jnp.bfloat16),
            pltpu.SemaphoreType.DMA((2,)),
        ]
    units = sources * (rows // BLK) * (W + R + 1)
    return pl.pallas_call(
        functools.partial(chunk_kernel, last, base),
        in_specs=[smem, vmem, hbm, hbm, hbm] + [hbm, vmem] * last,
        out_specs=[vmem] + [hbm] * (2 if last else 1) + [vmem],
        out_shape=[jax.ShapeDtypeStruct((sources, rows, HD), jnp.bfloat16)]
        + ([rounded] * 2 if last else [sums])
        + [
            jax.ShapeDtypeStruct((G, 2 * HD), jnp.float32),
        ],
        scratch_shapes=scratch,
        compiler_params=pltpu.CompilerParams(vmem_limit_bytes=VMEM_LIMIT),
        cost_estimate=pl.CostEstimate(
            flops=units * 16 * BLK * BLK * HD,
            bytes_accessed=total * BLK * HD * 16,
            transcendentals=units * BLK * BLK,
        ),
    )(table, glob, own, mate, pairs, *(before or ()))


def unpack_kernel(share, *refs):
    *in_refs, out_ref = refs
    rows = in_refs[0].shape[1]
    for chunk, in_ref in enumerate(in_refs):
        for index in range(in_ref.shape[0]):
            start = ((index % share) * CHUNKS + chunk) * rows
            head = index // share
            out_ref[start : start + rows, head * HD : (head + 1) * HD] = in_ref[index]


def unpack_queries(arrays, share):
    size, rows, _ = arrays[0].shape
    vmem = pl.BlockSpec(memory_space=pltpu.VMEM)
    shape = (share * CHUNKS * rows, size // share * HD)
    return pl.pallas_call(
        functools.partial(unpack_kernel, share),
        in_specs=[vmem] * len(arrays),
        out_specs=vmem,
        out_shape=jax.ShapeDtypeStruct(shape, jnp.bfloat16),
        compiler_params=pltpu.CompilerParams(vmem_limit_bytes=VMEM_LIMIT),
        cost_estimate=pl.CostEstimate(
            flops=0, bytes_accessed=shape[0] * shape[1] * 4, transcendentals=0
        ),
    )(*arrays)


def body_chunks(
    queries,
    keys,
    values,
    saved_output,
    grad_output,
    log_norm,
    global_keys,
    global_values,
    flow_links,
    glob_owner,
):
    size = lax.axis_size("seq")
    my_index = lax.axis_index("seq")
    tokens, features = queries.shape
    heads = features // HD
    blocks = tokens // BLK
    share = size // heads
    part = tokens // share
    sub = part // BLK
    mine = my_index % share

    owned = (glob_owner == my_index)[:, None, None]
    glob_pair = jnp.concatenate(
        [global_keys.reshape(G, heads, HD), global_values.reshape(G, heads, HD)], axis=2
    )
    glob_out = jnp.transpose(jnp.where(owned, glob_pair, jnp.bfloat16(0)), (1, 0, 2))
    glob_half = lax.psum_scatter(
        glob_out.reshape(size, G // share, 2 * HD), "seq", scatter_dimension=0, tiled=False
    )
    first = exchange(
        pack(queries, grad_output, saved_output, log_norm, 0, share, keys, values)
    )
    packed = pack(queries, grad_output, saved_output, log_norm, 1, share)
    packed, first, glob_half = lax.optimization_barrier((packed, first, glob_half))
    second = exchange(packed)
    mate = to_mate(first, 1, share)
    glob_mate = to_mate(glob_half, 1, share)
    glob_now = jnp.where(
        mine == 0,
        jnp.concatenate([glob_half, glob_mate], axis=0),
        jnp.concatenate([glob_mate, glob_half], axis=0),
    )

    count = size * sub
    order = jnp.arange(count, dtype=jnp.int32)
    my_blocks = (order // sub) * blocks + mine * sub + order % sub
    near = my_blocks[:, None] + jnp.arange(-1, 2, dtype=jnp.int32)[None, :]
    links = lax.dynamic_index_in_dim(
        flow_links.reshape(size, share, sub, R), mine, axis=1, keepdims=False
    ).reshape(count, R)
    wanted = jnp.concatenate([(near + size * blocks) % (size * blocks), links], axis=1)
    within = wanted % blocks
    offset = (within // sub - mine + share) % share
    table = (offset * count + (wanted // blocks) * sub + within % sub).astype(jnp.int32)
    tables = table.reshape(size, CHUNKS, -1)

    dq_first, sums, dglob = chunk_call(
        tables[:, 0].reshape(-1), glob_now, first, mate, first, part, part
    )
    dq_second, keep, give, dglob = chunk_call(
        tables[:, 1].reshape(-1), glob_now, first, mate, second, 0, part, (sums, dglob)
    )
    back_first = exchange(dq_first)
    dq_second, keep, give, dglob, back_first = lax.optimization_barrier(
        (dq_second, keep, give, dglob, back_first)
    )
    back_second = exchange(dq_second)
    dkv_sum = (keep.astype(jnp.float32) + to_mate(give, 1, share).astype(jnp.float32)).astype(
        jnp.bfloat16
    )
    dkv_sum, back_second = lax.optimization_barrier((dkv_sum, back_second))
    grad_keys, grad_values = unpair_heads(exchange(dkv_sum), share)
    grad_queries = unpack_queries((back_first, back_second), share)
    glob_parts = lax.all_gather(dglob, "seq", axis=0, tiled=False)
    glob_sum = jnp.sum(glob_parts.reshape(heads, share, G, 2, HD), axis=1)
    glob_grads = jnp.transpose(glob_sum, (2, 1, 0, 3)).reshape(2, G, features).astype(jnp.bfloat16)
    return (grad_queries, grad_keys, grad_values, glob_grads[0], glob_grads[1])


def body(queries, *rest):
    tokens, features = queries.shape
    share = lax.axis_size("seq") // (features // HD)
    if share == 2 and tokens % (share * CHUNKS * BLK) == 0:
        return body_chunks(queries, *rest)
    return body_shared(queries, *rest)


def solution(mesh):
    return jax.shard_map(
        body,
        mesh=mesh,
        in_specs=(
            P("seq", "tp"),
            P("seq", "tp"),
            P("seq", "tp"),
            P("seq", "tp"),
            P("seq", "tp"),
            P("tp", "seq"),
            P("seq", None, "tp"),
            P("seq", None, "tp"),
            P(),
            P(),
        ),
        out_specs=(P("seq", "tp"), P("seq", "tp"), P("seq", "tp"), P(None, "tp"), P(None, "tp")),
        check_vma=False,
    )
```

```python
import functools
import math

import jax
import jax.numpy as jnp
from jax import lax
from jax.experimental import pallas as pl
from jax.experimental.pallas import tpu as pltpu
from jax.sharding import PartitionSpec as P

HD = 128
BLK = 128
R = 3
G = 128
W = 3
FACTOR = HD ** (-0.5)
LOG2E = math.log2(math.e)
STAGE = 4


def pair_kernel(left_ref, right_ref, out_ref):
    heads = out_ref.shape[0]
    for head in range(heads):
        cols = slice(head * HD, (head + 1) * HD)
        out_ref[head, 0, :, :HD] = left_ref[:, cols]
        out_ref[head, 0, :, HD:] = right_ref[:, cols]


def pair_heads(left, right, share):
    tokens, features = left.shape
    heads = features // HD
    part = tokens // share
    rows = min(256, part)
    steps = part // rows
    out = pl.pallas_call(
        pair_kernel,
        grid=(share, steps),
        in_specs=[pl.BlockSpec((rows, features), lambda s, t: (s * steps + t, 0))] * 2,
        out_specs=pl.BlockSpec((heads, 1, rows, 2 * HD), lambda s, t: (0, s, t, 0)),
        out_shape=jax.ShapeDtypeStruct((heads, share, part, 2 * HD), left.dtype),
        cost_estimate=pl.CostEstimate(
            flops=0, bytes_accessed=4 * tokens * features * 2, transcendentals=0
        ),
    )(left, right)
    return out.reshape(heads * share, part, 2 * HD)


def unpair_kernel(in_ref, *out_refs):
    heads = in_ref.shape[0]
    for head in range(heads):
        cols = slice(head * HD, (head + 1) * HD)
        for which, out_ref in enumerate(out_refs):
            out_ref[:, cols] = in_ref[head, 0, :, which * HD : (which + 1) * HD]


def unpair_heads(mixed, share):
    parts, part, width = mixed.shape
    heads = parts // share
    count = width // HD
    rows = min(256, part)
    steps = part // rows
    shape = jax.ShapeDtypeStruct((share * part, heads * HD), mixed.dtype)
    return pl.pallas_call(
        unpair_kernel,
        grid=(share, steps),
        in_specs=[pl.BlockSpec((heads, 1, rows, width), lambda s, t: (0, s, t, 0))],
        out_specs=[pl.BlockSpec((rows, heads * HD), lambda s, t: (s * steps + t, 0))] * count,
        out_shape=[shape] * count,
        cost_estimate=pl.CostEstimate(
            flops=0, bytes_accessed=4 * parts * part * width, transcendentals=0
        ),
    )(mixed.reshape(heads, share, part, width))


def attention_kernel(
    table_ref, stats_ref, pair_ref, kv_ref, glob_ref, dq_ref, dkv_ref, dglob_ref, acc, stage, sems
):
    count, tile, _ = pair_ref.shape
    total = acc.shape[0]
    kinds = (W + R) * (BLK // tile)

    def clear(block, carry):
        acc[block] = jnp.zeros((tile, 2 * HD), jnp.float32)
        return carry

    lax.fori_loop(0, total, clear, 0)
    dglob_ref[...] = jnp.zeros_like(dglob_ref)
    zero = jnp.zeros((tile, HD), jnp.bfloat16)

    def one_block(block, carry):
        pair = pair_ref[block]
        mixed = jnp.concatenate(
            [
                jnp.concatenate([pair[:, :HD], zero], axis=1),
                jnp.concatenate([zero, pair[:, HD:]], axis=1),
            ],
            axis=0,
        )
        stats = stats_ref[block]
        norm = stats[0:1] * LOG2E
        delta = stats[1:2]
        places = [table_ref[block * kinds + kind] for kind in range(kinds)]
        rows = jnp.concatenate([kv_ref[place] for place in places] + [glob_ref[...]], axis=0)
        both = lax.dot_general(
            rows, mixed, (((1,), (1,)), ((), ())), preferred_element_type=jnp.float32
        )
        attend = jnp.exp2(both[:, :tile] * (FACTOR * LOG2E) - norm)
        grad_scores = attend * (both[:, tile:] - delta)
        attend_low = attend.astype(jnp.bfloat16)
        scores_low = grad_scores.astype(jnp.bfloat16)
        grad_kv = jnp.dot(
            jnp.concatenate([scores_low, attend_low], axis=1),
            mixed,
            preferred_element_type=jnp.float32,
        )
        for kind, place in enumerate(places):
            acc[place] += grad_kv[kind * tile : (kind + 1) * tile]
        dglob_ref[...] += grad_kv[kinds * tile :]
        grad_q = lax.dot_general(
            scores_low, rows[:, :HD], (((0,), (0,)), ((), ())), preferred_element_type=jnp.float32
        )
        dq_ref[block] = (grad_q * FACTOR).astype(jnp.bfloat16)
        return carry

    lax.fori_loop(0, count, one_block, 0)
    dglob_ref[:, :HD] = dglob_ref[:, :HD] * FACTOR

    def copy_out(step, slot):
        return pltpu.make_async_copy(
            stage.at[slot], dkv_ref.at[pl.ds(step * STAGE, STAGE)], sems.at[slot]
        )

    steps = total // STAGE
    for step in range(steps):
        slot = step % 2
        if step >= 2:
            copy_out(step - 2, slot).wait()
        part = acc[step * STAGE : (step + 1) * STAGE]
        stage[slot, :, :, :HD] = (part[:, :, :HD] * FACTOR).astype(jnp.bfloat16)
        stage[slot, :, :, HD:] = part[:, :, HD:].astype(jnp.bfloat16)
        copy_out(step, slot).start()
    for step in range(max(0, steps - 2), steps):
        copy_out(step, step % 2).wait()


def attention(table, stats, pairs, kv, glob):
    count, tile, _ = pairs.shape
    total = kv.shape[0]
    vmem = pl.BlockSpec(memory_space=pltpu.VMEM)
    return pl.pallas_call(
        attention_kernel,
        in_specs=[pl.BlockSpec(memory_space=pltpu.SMEM), vmem, vmem, vmem, vmem],
        out_specs=[vmem, pl.BlockSpec(memory_space=pl.ANY), vmem],
        out_shape=[
            jax.ShapeDtypeStruct((count, tile, HD), jnp.bfloat16),
            jax.ShapeDtypeStruct((total, tile, 2 * HD), jnp.bfloat16),
            jax.ShapeDtypeStruct((G, 2 * HD), jnp.float32),
        ],
        scratch_shapes=[
            pltpu.VMEM((total, tile, 2 * HD), jnp.float32),
            pltpu.VMEM((2, STAGE, tile, 2 * HD), jnp.bfloat16),
            pltpu.SemaphoreType.DMA((2,)),
        ],
        compiler_params=pltpu.CompilerParams(vmem_limit_bytes=60 * 1024 * 1024),
        cost_estimate=pl.CostEstimate(
            flops=count * (W + R + 1) * 10 * tile * BLK * HD,
            bytes_accessed=(total * 8 + count * 6) * tile * HD,
            transcendentals=count * (W + R + 1) * tile * BLK,
        ),
    )(table, stats, pairs, kv, glob)


def exchange(array):
    return lax.all_to_all(array, "seq", split_axis=0, concat_axis=0, tiled=True)


def to_mate(array, step, share):
    size = lax.axis_size("seq")
    return lax.ppermute(
        array, "seq", [(i, i - i % share + (i + step) % share) for i in range(size)]
    )


def body_shared(
    queries,
    keys,
    values,
    saved_output,
    grad_output,
    log_norm,
    global_keys,
    global_values,
    flow_links,
    glob_owner,
):
    size = lax.axis_size("seq")
    tokens, features = queries.shape
    heads = features // HD
    blocks = tokens // BLK
    share = size // heads
    part = tokens // share
    tile = min(BLK, part)
    sub = part // tile
    pieces = BLK // tile
    count = size * sub
    mine = lax.axis_index("seq") % share

    kv_own = exchange(pair_heads(keys, values, share))
    glob_pair = jnp.concatenate(
        [global_keys.reshape(G, heads, HD), global_values.reshape(G, heads, HD)], axis=2
    )
    glob_out = jnp.repeat(jnp.transpose(glob_pair, (1, 0, 2)), share, axis=0)
    glob_in = exchange(glob_out)
    product = grad_output.astype(jnp.float32) * saved_output.astype(jnp.float32)
    delta = jnp.sum(product.reshape(tokens, heads, HD), axis=2).T
    stats_out = jnp.stack(
        [log_norm.reshape(size, part), delta.reshape(size, part)], axis=1
    )
    stats_in = exchange(stats_out)
    pairs = exchange(pair_heads(queries, grad_output, share))

    owners = jnp.arange(size, dtype=jnp.int32)[:, None] == glob_owner[None, :]
    glob_now = jnp.sum(
        jnp.where(owners[:, :, None], glob_in.astype(jnp.float32), 0.0), axis=0
    ).astype(jnp.bfloat16)
    stats = jnp.transpose(stats_in.reshape(size, 2, sub, tile), (0, 2, 1, 3)).reshape(
        count, 2, tile
    )
    kv = jnp.concatenate(
        [kv_own] + [to_mate(kv_own, share - step, share) for step in range(1, share)], axis=0
    ).reshape(share * count, tile, 2 * HD)

    order = jnp.arange(count, dtype=jnp.int32)
    my_blocks = (order // sub) * blocks + (mine * sub + order % sub) // pieces
    near = my_blocks[:, None] + jnp.arange(-1, 2, dtype=jnp.int32)[None, :]
    wanted = jnp.concatenate(
        [(near + size * blocks) % (size * blocks), flow_links[my_blocks]], axis=1
    )
    within = (wanted % blocks)[:, :, None] * pieces + jnp.arange(pieces, dtype=jnp.int32)
    offset = (within // sub - mine + share) % share
    table = offset * count + (wanted // blocks)[:, :, None] * sub + within % sub

    dq, dkv, dglob = attention(
        table.reshape(-1).astype(jnp.int32),
        stats,
        pairs.reshape(count, tile, 2 * HD),
        kv,
        glob_now,
    )
    dq_back = exchange(dq.reshape(size, part, HD))
    dkv = dkv.reshape(share, size, part, 2 * HD)
    dkv_sum = dkv[0].astype(jnp.float32)
    for step in range(1, share):
        dkv_sum = dkv_sum + to_mate(dkv[step], step, share).astype(jnp.float32)
    dkv_back = exchange(dkv_sum.astype(jnp.bfloat16))
    glob_parts = lax.all_gather(dglob, "seq", axis=0, tiled=False)
    glob_sum = jnp.sum(glob_parts.reshape(heads, share, G, 2, HD), axis=1)
    glob_grads = jnp.transpose(glob_sum, (2, 1, 0, 3)).reshape(2, G, features).astype(jnp.bfloat16)

    (grad_queries,) = unpair_heads(dq_back, share)
    grad_keys, grad_values = unpair_heads(dkv_back, share)
    return (grad_queries, grad_keys, grad_values, glob_grads[0], glob_grads[1])


CHUNKS = ((0, 6), (6, 2))
UNROLL = (1, 4)
VMEM_LIMIT = 60 * 1024 * 1024


def pad_of(some):
    return (2 * some + 7) // 8 * 8


def split_two(row):
    high = row.astype(jnp.bfloat16).astype(jnp.float32)
    return jnp.concatenate([high, row - high], axis=1)


def pack_kernel(query_ref, grad_ref, saved_ref, norm_ref, out_ref):
    rows = query_ref.shape[0]
    for head in range(out_ref.shape[1]):
        cols = slice(head * HD, (head + 1) * HD)
        query = query_ref[:, cols]
        grad = grad_ref[:, cols]
        product = grad.astype(jnp.float32) * saved_ref[:, cols].astype(jnp.float32)
        delta = jnp.sum(product.T, axis=0, keepdims=True)
        norm = norm_ref[head : head + 1, :]
        stats = []
        for block in range(rows // BLK):
            lanes = slice(block * BLK, (block + 1) * BLK)
            stats += [split_two(norm[:, lanes]), split_two(delta[:, lanes])]
        pad = out_ref.shape[2] - rows
        if len(stats) < pad:
            stats.append(jnp.zeros((pad - len(stats), 2 * HD), jnp.float32))
        stats = jnp.concatenate(stats, axis=0).astype(jnp.bfloat16)
        for half in range(2):
            out_ref[half, head, :rows, :HD] = query
            out_ref[half, head, :rows, HD:] = grad
            out_ref[half, head, rows:, :] = stats


def pack_queries(queries, grad_output, saved_output, log_norm, first, some):
    tokens, features = queries.shape
    heads = features // HD
    rows = some * BLK
    place = first // some
    spec = pl.BlockSpec((rows, features), lambda i: (place, 0))
    shape = (2, heads, rows + pad_of(some), 2 * HD)
    out = pl.pallas_call(
        pack_kernel,
        grid=(1,),
        in_specs=[spec] * 3 + [pl.BlockSpec((heads, rows), lambda i: (0, place))],
        out_specs=pl.BlockSpec(shape, lambda i: (0, 0, 0, 0)),
        out_shape=jax.ShapeDtypeStruct(shape, jnp.bfloat16),
        compiler_params=pltpu.CompilerParams(vmem_limit_bytes=VMEM_LIMIT),
        cost_estimate=pl.CostEstimate(
            flops=0, bytes_accessed=rows * features * 14, transcendentals=0
        ),
    )(queries, grad_output, saved_output, log_norm)
    return out.reshape(2 * heads, rows + pad_of(some), 2 * HD)


def pack_keys_kernel(mine_ref, key_ref, value_ref, glob_key_ref, glob_value_ref, *out_refs):
    tokens = key_ref.shape[0]
    chips = len(out_refs)
    chip, core = mine_ref[0] // 2, mine_ref[0] % 2
    for step, out_ref in enumerate(out_refs):
        there = lax.rem(chip + step, chips)
        for side in range(2):
            head = 2 * there + (core if side == 0 else 1 - core)
            cols = pl.ds(pl.multiple_of(head * HD, HD), HD)
            start = side * (tokens + G)
            out_ref[start : start + tokens, :HD] = key_ref[:, cols]
            out_ref[start : start + tokens, HD:] = value_ref[:, cols]
            out_ref[start + tokens : start + tokens + G, :HD] = glob_key_ref[:, cols]
            out_ref[start + tokens : start + tokens + G, HD:] = glob_value_ref[:, cols]


def pack_keys(mine, keys, values, glob_keys, glob_values):
    tokens, features = keys.shape
    chips = features // HD // 2
    vmem = pl.BlockSpec(memory_space=pltpu.VMEM)
    return pl.pallas_call(
        pack_keys_kernel,
        in_specs=[pl.BlockSpec(memory_space=pltpu.SMEM)] + [vmem] * 4,
        out_specs=[vmem] * chips,
        out_shape=[jax.ShapeDtypeStruct((2 * (tokens + G), 2 * HD), jnp.bfloat16)] * chips,
        compiler_params=pltpu.CompilerParams(vmem_limit_bytes=VMEM_LIMIT),
        cost_estimate=pl.CostEstimate(
            flops=0, bytes_accessed=(tokens + G) * features * 8, transcendentals=0
        ),
    )(mine, keys, values, glob_keys, glob_values)


def pair_grads(pair, stats, rows, valid):
    zero = jnp.zeros((BLK, HD), jnp.bfloat16)
    mixed = jnp.concatenate(
        [
            jnp.concatenate([pair[:, :HD], zero], axis=1),
            jnp.concatenate([zero, pair[:, HD:]], axis=1),
        ],
        axis=0,
    )
    norm = (stats[0:1, :HD] + stats[0:1, HD:]) * LOG2E
    delta = stats[1:2, :HD] + stats[1:2, HD:]
    rows = jnp.concatenate(rows, axis=0) if len(rows) > 1 else rows[0]
    both = lax.dot_general(
        rows, mixed, (((1,), (1,)), ((), ())), preferred_element_type=jnp.float32
    )
    attend = jnp.exp2(both[:, :HD] * (FACTOR * LOG2E) - norm)
    parts = []
    for kind, known in enumerate(valid):
        part = attend[kind * BLK : (kind + 1) * BLK]
        parts.append(part if known is None else jnp.where(known, part, 0.0))
    attend = jnp.concatenate(parts, axis=0) if len(parts) > 1 else parts[0]
    grad_scores = attend * (both[:, HD:] - delta)
    scores_low = grad_scores.astype(jnp.bfloat16)
    grad_kv = jnp.dot(
        jnp.concatenate([scores_low, attend.astype(jnp.bfloat16)], axis=1),
        mixed,
        preferred_element_type=jnp.float32,
    )
    grad_q = lax.dot_general(
        scores_low, rows[:, :HD], (((0,), (0,)), ((), ())), preferred_element_type=jnp.float32
    )
    return grad_kv, grad_q * FACTOR


def chunk_kernel(chunk, heads, table_ref, glob_ref, pair_ref, *refs):
    kv_refs, refs = refs[:heads], refs[heads:]
    last = chunk == len(CHUNKS) - 1
    some = CHUNKS[chunk][1]
    if last:
        before_ref, glob_before_ref, dq_ref = refs[:3]
        out_refs, refs = refs[3 : 3 + heads // 2], refs[3 + heads // 2 :]
        dglob_ref, kv, pairs, acc, sems, before, stage, out_sems = refs
    else:
        dq_ref, sum_ref, dglob_ref, kv, pairs, acc, sems = refs
    sources = pairs.shape[0]
    total = acc.shape[0]
    blocks = total // heads
    own_kinds = W + R
    own_base = heads * some * own_kinds
    rim_base = own_base + heads * some * R
    half = table_ref[rim_base + 2]
    copies = [
        pltpu.make_async_copy(
            kv_ref.at[pl.ds(step % 2 * (blocks * BLK + G), blocks * BLK), :],
            kv.at[step],
            sems.at[step],
        )
        for step, kv_ref in enumerate(kv_refs)
    ]
    copies.append(pltpu.make_async_copy(pair_ref, pairs, sems.at[heads]))
    for copy in copies:
        copy.start()
    if last:
        earlier = pltpu.make_async_copy(before_ref, before, sems.at[heads + 1])
        earlier.start()
        dglob_ref[...] = glob_before_ref[...]
    else:
        dglob_ref[...] = jnp.zeros_like(dglob_ref)

    def clear(block, carry):
        acc[block] = jnp.zeros((BLK, 2 * HD), jnp.float32)
        return carry

    lax.fori_loop(0, total, clear, 0)
    for copy in copies:
        copy.wait()

    def meet(source, inner, wanted, with_glob):
        lines = slice(inner * BLK, (inner + 1) * BLK)
        stats = pairs[source, some * BLK :, :].astype(jnp.float32)
        places = [jnp.maximum(place, 0) for place in wanted]
        rows = [
            kv[place // blocks, pl.ds(pl.multiple_of((place % blocks) * BLK, BLK), BLK), :]
            for place in places
        ]
        valid = [place >= 0 for place in wanted]
        if with_glob:
            rows.append(glob_ref[...])
            valid.append(None)
        grad_kv, grad_q = pair_grads(
            pairs[source, lines, :], stats[2 * inner : 2 * inner + 2], rows, valid
        )
        for kind, place in enumerate(places):
            acc[place] += grad_kv[kind * BLK : (kind + 1) * BLK]
        if with_glob:
            dglob_ref[...] += grad_kv[len(places) * BLK :]
        return lines, grad_q

    def one_own(index, carry):
        source = half * heads + index
        for inner in range(some):
            entry = (index * some + inner) * own_kinds
            wanted = [table_ref[entry + kind] for kind in range(own_kinds)]
            lines, grad_q = meet(source, inner, wanted, True)
            dq_ref[source, lines, :] = grad_q.astype(jnp.bfloat16)
        return carry

    def one_other(index, carry):
        source = (1 - half) * heads + index
        for inner in range(some):
            entry = own_base + (index * some + inner) * R
            wanted = [table_ref[entry + kind] for kind in range(R)]
            lines, grad_q = meet(source, inner, wanted, True)
            dq_ref[source, lines, :] = grad_q.astype(jnp.bfloat16)
        return carry

    lax.fori_loop(0, heads, one_own, 0, unroll=UNROLL[chunk])
    lax.fori_loop(0, heads, one_other, 0, unroll=UNROLL[chunk])
    rims = []
    if chunk == 0:
        rims.append((0, 0, rim_base))
    if last:
        rims.append((heads - 1, some - 1, rim_base + 1))
    for index, inner, entry in rims:
        source = (1 - half) * heads + index
        lines, grad_q = meet(source, inner, [table_ref[entry]], False)
        dq_ref[source, lines, :] = (
            dq_ref[source, lines, :].astype(jnp.float32) + grad_q
        ).astype(jnp.bfloat16)
    if not last:
        leave = pltpu.make_async_copy(acc, sum_ref, sems.at[heads + 1])
        leave.start()
        leave.wait()
        return
    dglob_ref[:, :HD] = dglob_ref[:, :HD] * FACTOR
    earlier.wait()

    def copy_out(step):
        slot = step % 2
        out = out_refs[step // 2].at[pl.ds(step % 2 * (blocks * BLK), blocks * BLK), :]
        return pltpu.make_async_copy(stage.at[slot], out, out_sems.at[slot])

    for step in range(heads):
        if step >= 2:
            copy_out(step - 2).wait()
        for inner in range(blocks):
            value = acc[step * blocks + inner] + before[step * blocks + inner]
            lines = slice(inner * BLK, (inner + 1) * BLK)
            stage[step % 2, lines, :HD] = (value[:, :HD] * FACTOR).astype(jnp.bfloat16)
            stage[step % 2, lines, HD:] = value[:, HD:].astype(jnp.bfloat16)
        copy_out(step).start()
    for step in range(max(0, heads - 2), heads):
        copy_out(step).wait()


def chunk_call(chunk, table, glob, pairs, kv, before=()):
    sources = pairs.shape[0]
    heads = len(kv)
    rows = CHUNKS[chunk][1] * BLK
    tokens = kv[0].shape[0] // 2 - G
    total = heads * (tokens // BLK)
    last = chunk == len(CHUNKS) - 1
    vmem = pl.BlockSpec(memory_space=pltpu.VMEM)
    smem = pl.BlockSpec(memory_space=pltpu.SMEM)
    hbm = pl.BlockSpec(memory_space=pl.ANY)
    sums = jax.ShapeDtypeStruct((total, BLK, 2 * HD), jnp.float32)
    rounded = jax.ShapeDtypeStruct((2 * tokens, 2 * HD), jnp.bfloat16)
    scratch = [
        pltpu.VMEM((heads, tokens, 2 * HD), jnp.bfloat16),
        pltpu.VMEM(pairs.shape, jnp.bfloat16),
        pltpu.VMEM(sums.shape, jnp.float32),
        pltpu.SemaphoreType.DMA((heads + 2,)),
    ]
    if last:
        scratch += [
            pltpu.VMEM(sums.shape, jnp.float32),
            pltpu.VMEM((2, tokens, 2 * HD), jnp.bfloat16),
            pltpu.SemaphoreType.DMA((2,)),
        ]
    units = heads * (rows // BLK) * (W + 2 * R + 2)
    return pl.pallas_call(
        functools.partial(chunk_kernel, chunk, heads),
        in_specs=[smem, vmem, hbm] + [hbm] * heads + [hbm, vmem] * last,
        out_specs=[vmem] + [hbm] * (heads // 2 if last else 1) + [vmem],
        out_shape=[jax.ShapeDtypeStruct((sources, rows, HD), jnp.bfloat16)]
        + ([rounded] * (heads // 2) if last else [sums])
        + [jax.ShapeDtypeStruct((G, 2 * HD), jnp.float32)],
        scratch_shapes=scratch,
        compiler_params=pltpu.CompilerParams(vmem_limit_bytes=VMEM_LIMIT),
        cost_estimate=pl.CostEstimate(
            flops=units * 16 * BLK * BLK * HD,
            bytes_accessed=total * BLK * HD * 16,
            transcendentals=units * BLK * BLK,
        ),
    )(table, glob, pairs, *kv, *before)


def unpack_queries_kernel(*refs):
    *in_refs, out_ref = refs
    heads = in_refs[0].shape[0] // 2
    for (first, some), in_ref in zip(CHUNKS, in_refs):
        for head in range(heads):
            total = in_ref[head].astype(jnp.float32) + in_ref[heads + head].astype(jnp.float32)
            out_ref[first * BLK : (first + some) * BLK, head * HD : (head + 1) * HD] = total.astype(
                jnp.bfloat16
            )


def unpack_queries(arrays):
    shape = (sum(array.shape[1] for array in arrays), arrays[0].shape[0] // 2 * HD)
    vmem = pl.BlockSpec(memory_space=pltpu.VMEM)
    return pl.pallas_call(
        unpack_queries_kernel,
        in_specs=[vmem] * len(arrays),
        out_specs=vmem,
        out_shape=jax.ShapeDtypeStruct(shape, jnp.bfloat16),
        compiler_params=pltpu.CompilerParams(vmem_limit_bytes=VMEM_LIMIT),
        cost_estimate=pl.CostEstimate(
            flops=0, bytes_accessed=shape[0] * shape[1] * 6, transcendentals=0
        ),
    )(*arrays)


def unpack_keys_kernel(mine_ref, *refs):
    *in_refs, dk_ref, dv_ref = refs
    chips = len(in_refs) // 2
    chip, core = mine_ref[0] // 2, mine_ref[0] % 2
    for step, in_ref in enumerate(in_refs):
        there = lax.rem(chip + step // 2, chips)
        head = 2 * there + (core if step % 2 == 0 else 1 - core)
        cols = pl.ds(pl.multiple_of(head * HD, HD), HD)
        dk_ref[:, cols] = in_ref[:, :HD]
        dv_ref[:, cols] = in_ref[:, HD:]


def unpack_keys(mine, arrays):
    tokens = arrays[0].shape[0] // 2
    heads = len(arrays)
    rows = tokens // 2
    shape = jax.ShapeDtypeStruct((tokens, heads * HD), jnp.bfloat16)
    sides = [
        pl.BlockSpec((rows, 2 * HD), lambda i: (i, 0)),
        pl.BlockSpec((rows, 2 * HD), lambda i: (2 + i, 0)),
    ]
    return pl.pallas_call(
        unpack_keys_kernel,
        grid=(2,),
        in_specs=[pl.BlockSpec(memory_space=pltpu.SMEM)] + sides * (heads // 2),
        out_specs=[pl.BlockSpec((rows, heads * HD), lambda i: (i, 0))] * 2,
        out_shape=[shape] * 2,
        compiler_params=pltpu.CompilerParams(vmem_limit_bytes=VMEM_LIMIT),
        cost_estimate=pl.CostEstimate(
            flops=0, bytes_accessed=tokens * heads * HD * 8, transcendentals=0
        ),
    )(mine, *arrays)


def body_halves(
    queries,
    keys,
    values,
    saved_output,
    grad_output,
    log_norm,
    global_keys,
    global_values,
    flow_links,
    glob_owner,
):
    size = lax.axis_size("seq")
    my_index = lax.axis_index("seq")
    tokens, features = queries.shape
    heads = features // HD
    blocks = tokens // BLK
    count = heads * blocks
    half = my_index // heads
    mine = my_index % heads
    mine_one = mine.astype(jnp.int32).reshape(1)

    chips = heads // 2

    def turn(array, step):
        pairs = [
            (i, i - i % heads + (i % heads // 2 + step) % chips * 2 + i % 2) for i in range(size)
        ]
        return lax.ppermute(array, "seq", pairs) if step % chips else array

    def over(array):
        return lax.ppermute(array, "seq", [(i, i ^ 1) for i in range(size)])

    first = exchange(pack_queries(queries, grad_output, saved_output, log_norm, *CHUNKS[0]))
    owned = (glob_owner == my_index)[:, None]
    slabs = pack_keys(
        mine_one,
        keys,
        values,
        jnp.where(owned, global_keys[0], jnp.bfloat16(0)),
        jnp.where(owned, global_values[0], jnp.bfloat16(0)),
    )
    near_kv = [turn(slab, step) for step, slab in enumerate(slabs)]
    kv = [piece for slab in near_kv for piece in (slab, over(slab))]
    packed = pack_queries(queries, grad_output, saved_output, log_norm, *CHUNKS[1])
    packed, first, *kv = lax.optimization_barrier((packed, first, *kv))
    second = exchange(packed)
    glob_now = functools.reduce(
        jnp.add,
        [
            piece[tokens + step % 2 * (tokens + G) :][:G].astype(jnp.float32)
            for step, piece in enumerate(kv)
        ],
    ).astype(jnp.bfloat16)

    def places(wanted):
        here = wanted - half * count
        owner = here // blocks
        step = (mine // 2 - owner // 2 + chips) % chips * 2 + (mine + owner) % 2
        return jnp.where((here >= 0) & (here < count), step * blocks + here % blocks, -1)

    links = flow_links.reshape(2, count, R)
    my_links = lax.dynamic_index_in_dim(links, half, axis=0, keepdims=False)
    other_links = lax.dynamic_index_in_dim(links, 1 - half, axis=0, keepdims=False)
    order = half * count + jnp.arange(count, dtype=jnp.int32)
    near = (order[:, None] + jnp.arange(-1, 2, dtype=jnp.int32) + 2 * count) % (2 * count)
    own = places(jnp.concatenate([near, my_links], axis=1)).reshape(heads, blocks, -1)
    other = places(other_links).reshape(heads, blocks, -1)
    ends = places(jnp.stack([half * count + count - 1, half * count]))
    tail = jnp.concatenate([ends, half.reshape(1)])
    tables = [
        jnp.concatenate(
            [part[:, first : first + some].reshape(-1) for part in (own, other)] + [tail]
        ).astype(jnp.int32)
        for first, some in CHUNKS
    ]

    dq_first, sums, dglob = chunk_call(0, tables[0], glob_now, first, kv)
    back_first = exchange(dq_first)
    dq_second, *slabs, dglob = chunk_call(1, tables[1], glob_now, second, kv, (sums, dglob))
    dq_second, back_first, dglob = lax.optimization_barrier((dq_second, back_first, dglob))
    slabs = [turn(slab, chips - step) for step, slab in enumerate(slabs)]
    dq_second, slabs[2] = lax.optimization_barrier((dq_second, slabs[2]))
    back_second = exchange(dq_second)
    grad_keys, grad_values = unpack_keys(
        mine_one, [piece for slab in slabs for piece in (slab, over(slab))]
    )
    grad_queries = unpack_queries((back_first, back_second))
    held = (glob_owner // heads == half)[:, None]
    glob_parts = lax.all_gather(
        jnp.where(held, dglob, 0.0).astype(jnp.bfloat16), "seq", axis=0, tiled=False
    ).astype(jnp.float32)
    glob_sum = (glob_parts[:heads] + glob_parts[heads:]).reshape(heads, G, 2, HD)
    glob_grads = jnp.transpose(glob_sum, (2, 1, 0, 3)).reshape(2, G, features).astype(jnp.bfloat16)
    return (grad_queries, grad_keys, grad_values, glob_grads[0], glob_grads[1])


def body(queries, *rest):
    tokens, features = queries.shape
    blocks = sum(some for _, some in CHUNKS)
    if lax.axis_size("seq") == 2 * (features // HD) and tokens == blocks * BLK:
        return body_halves(queries, *rest)
    return body_shared(queries, *rest)


def solution(mesh):
    return jax.shard_map(
        body,
        mesh=mesh,
        in_specs=(
            P("seq", "tp"),
            P("seq", "tp"),
            P("seq", "tp"),
            P("seq", "tp"),
            P("seq", "tp"),
            P("tp", "seq"),
            P("seq", None, "tp"),
            P("seq", None, "tp"),
            P(),
            P(),
        ),
        out_specs=(P("seq", "tp"), P("seq", "tp"), P("seq", "tp"), P(None, "tp"), P(None, "tp")),
        check_vma=False,
    )
```

```python
import functools
import math

import jax
import jax.numpy as jnp
from jax import lax
from jax.experimental import pallas as pl
from jax.experimental.pallas import tpu as pltpu
from jax.sharding import PartitionSpec as P

HD = 128
BLK = 128
R = 3
G = 128
W = 3
FACTOR = HD ** (-0.5)
LOG2E = math.log2(math.e)
STAGE = 4


def pair_kernel(left_ref, right_ref, out_ref):
    heads = out_ref.shape[0]
    for head in range(heads):
        cols = slice(head * HD, (head + 1) * HD)
        out_ref[head, 0, :, :HD] = left_ref[:, cols]
        out_ref[head, 0, :, HD:] = right_ref[:, cols]


def pair_heads(left, right, share):
    tokens, features = left.shape
    heads = features // HD
    part = tokens // share
    rows = min(256, part)
    steps = part // rows
    out = pl.pallas_call(
        pair_kernel,
        grid=(share, steps),
        in_specs=[pl.BlockSpec((rows, features), lambda s, t: (s * steps + t, 0))] * 2,
        out_specs=pl.BlockSpec((heads, 1, rows, 2 * HD), lambda s, t: (0, s, t, 0)),
        out_shape=jax.ShapeDtypeStruct((heads, share, part, 2 * HD), left.dtype),
        cost_estimate=pl.CostEstimate(
            flops=0, bytes_accessed=4 * tokens * features * 2, transcendentals=0
        ),
    )(left, right)
    return out.reshape(heads * share, part, 2 * HD)


def unpair_kernel(in_ref, *out_refs):
    heads = in_ref.shape[0]
    for head in range(heads):
        cols = slice(head * HD, (head + 1) * HD)
        for which, out_ref in enumerate(out_refs):
            out_ref[:, cols] = in_ref[head, 0, :, which * HD : (which + 1) * HD]


def unpair_heads(mixed, share):
    parts, part, width = mixed.shape
    heads = parts // share
    count = width // HD
    rows = min(256, part)
    steps = part // rows
    shape = jax.ShapeDtypeStruct((share * part, heads * HD), mixed.dtype)
    return pl.pallas_call(
        unpair_kernel,
        grid=(share, steps),
        in_specs=[pl.BlockSpec((heads, 1, rows, width), lambda s, t: (0, s, t, 0))],
        out_specs=[pl.BlockSpec((rows, heads * HD), lambda s, t: (s * steps + t, 0))] * count,
        out_shape=[shape] * count,
        cost_estimate=pl.CostEstimate(
            flops=0, bytes_accessed=4 * parts * part * width, transcendentals=0
        ),
    )(mixed.reshape(heads, share, part, width))


def attention_kernel(
    table_ref, stats_ref, pair_ref, kv_ref, glob_ref, dq_ref, dkv_ref, dglob_ref, acc, stage, sems
):
    count, tile, _ = pair_ref.shape
    total = acc.shape[0]
    kinds = (W + R) * (BLK // tile)

    def clear(block, carry):
        acc[block] = jnp.zeros((tile, 2 * HD), jnp.float32)
        return carry

    lax.fori_loop(0, total, clear, 0)
    dglob_ref[...] = jnp.zeros_like(dglob_ref)
    zero = jnp.zeros((tile, HD), jnp.bfloat16)

    def one_block(block, carry):
        pair = pair_ref[block]
        mixed = jnp.concatenate(
            [
                jnp.concatenate([pair[:, :HD], zero], axis=1),
                jnp.concatenate([zero, pair[:, HD:]], axis=1),
            ],
            axis=0,
        )
        stats = stats_ref[block]
        norm = stats[0:1] * LOG2E
        delta = stats[1:2]
        places = [table_ref[block * kinds + kind] for kind in range(kinds)]
        rows = jnp.concatenate([kv_ref[place] for place in places] + [glob_ref[...]], axis=0)
        both = lax.dot_general(
            rows, mixed, (((1,), (1,)), ((), ())), preferred_element_type=jnp.float32
        )
        attend = jnp.exp2(both[:, :tile] * (FACTOR * LOG2E) - norm)
        grad_scores = attend * (both[:, tile:] - delta)
        attend_low = attend.astype(jnp.bfloat16)
        scores_low = grad_scores.astype(jnp.bfloat16)
        grad_kv = jnp.dot(
            jnp.concatenate([scores_low, attend_low], axis=1),
            mixed,
            preferred_element_type=jnp.float32,
        )
        for kind, place in enumerate(places):
            acc[place] += grad_kv[kind * tile : (kind + 1) * tile]
        dglob_ref[...] += grad_kv[kinds * tile :]
        grad_q = lax.dot_general(
            scores_low, rows[:, :HD], (((0,), (0,)), ((), ())), preferred_element_type=jnp.float32
        )
        dq_ref[block] = (grad_q * FACTOR).astype(jnp.bfloat16)
        return carry

    lax.fori_loop(0, count, one_block, 0)
    dglob_ref[:, :HD] = dglob_ref[:, :HD] * FACTOR

    def copy_out(step, slot):
        return pltpu.make_async_copy(
            stage.at[slot], dkv_ref.at[pl.ds(step * STAGE, STAGE)], sems.at[slot]
        )

    steps = total // STAGE
    for step in range(steps):
        slot = step % 2
        if step >= 2:
            copy_out(step - 2, slot).wait()
        part = acc[step * STAGE : (step + 1) * STAGE]
        stage[slot, :, :, :HD] = (part[:, :, :HD] * FACTOR).astype(jnp.bfloat16)
        stage[slot, :, :, HD:] = part[:, :, HD:].astype(jnp.bfloat16)
        copy_out(step, slot).start()
    for step in range(max(0, steps - 2), steps):
        copy_out(step, step % 2).wait()


def attention(table, stats, pairs, kv, glob):
    count, tile, _ = pairs.shape
    total = kv.shape[0]
    vmem = pl.BlockSpec(memory_space=pltpu.VMEM)
    return pl.pallas_call(
        attention_kernel,
        in_specs=[pl.BlockSpec(memory_space=pltpu.SMEM), vmem, vmem, vmem, vmem],
        out_specs=[vmem, pl.BlockSpec(memory_space=pl.ANY), vmem],
        out_shape=[
            jax.ShapeDtypeStruct((count, tile, HD), jnp.bfloat16),
            jax.ShapeDtypeStruct((total, tile, 2 * HD), jnp.bfloat16),
            jax.ShapeDtypeStruct((G, 2 * HD), jnp.float32),
        ],
        scratch_shapes=[
            pltpu.VMEM((total, tile, 2 * HD), jnp.float32),
            pltpu.VMEM((2, STAGE, tile, 2 * HD), jnp.bfloat16),
            pltpu.SemaphoreType.DMA((2,)),
        ],
        compiler_params=pltpu.CompilerParams(vmem_limit_bytes=60 * 1024 * 1024),
        cost_estimate=pl.CostEstimate(
            flops=count * (W + R + 1) * 10 * tile * BLK * HD,
            bytes_accessed=(total * 8 + count * 6) * tile * HD,
            transcendentals=count * (W + R + 1) * tile * BLK,
        ),
    )(table, stats, pairs, kv, glob)


def exchange(array):
    return lax.all_to_all(array, "seq", split_axis=0, concat_axis=0, tiled=True)


def to_mate(array, step, share):
    size = lax.axis_size("seq")
    return lax.ppermute(
        array, "seq", [(i, i - i % share + (i + step) % share) for i in range(size)]
    )


def body_shared(
    queries,
    keys,
    values,
    saved_output,
    grad_output,
    log_norm,
    global_keys,
    global_values,
    flow_links,
    glob_owner,
):
    size = lax.axis_size("seq")
    tokens, features = queries.shape
    heads = features // HD
    blocks = tokens // BLK
    share = size // heads
    part = tokens // share
    tile = min(BLK, part)
    sub = part // tile
    pieces = BLK // tile
    count = size * sub
    mine = lax.axis_index("seq") % share

    kv_own = exchange(pair_heads(keys, values, share))
    glob_pair = jnp.concatenate(
        [global_keys.reshape(G, heads, HD), global_values.reshape(G, heads, HD)], axis=2
    )
    glob_out = jnp.repeat(jnp.transpose(glob_pair, (1, 0, 2)), share, axis=0)
    glob_in = exchange(glob_out)
    product = grad_output.astype(jnp.float32) * saved_output.astype(jnp.float32)
    delta = jnp.sum(product.reshape(tokens, heads, HD), axis=2).T
    stats_out = jnp.stack(
        [log_norm.reshape(size, part), delta.reshape(size, part)], axis=1
    )
    stats_in = exchange(stats_out)
    pairs = exchange(pair_heads(queries, grad_output, share))

    owners = jnp.arange(size, dtype=jnp.int32)[:, None] == glob_owner[None, :]
    glob_now = jnp.sum(
        jnp.where(owners[:, :, None], glob_in.astype(jnp.float32), 0.0), axis=0
    ).astype(jnp.bfloat16)
    stats = jnp.transpose(stats_in.reshape(size, 2, sub, tile), (0, 2, 1, 3)).reshape(
        count, 2, tile
    )
    kv = jnp.concatenate(
        [kv_own] + [to_mate(kv_own, share - step, share) for step in range(1, share)], axis=0
    ).reshape(share * count, tile, 2 * HD)

    order = jnp.arange(count, dtype=jnp.int32)
    my_blocks = (order // sub) * blocks + (mine * sub + order % sub) // pieces
    near = my_blocks[:, None] + jnp.arange(-1, 2, dtype=jnp.int32)[None, :]
    wanted = jnp.concatenate(
        [(near + size * blocks) % (size * blocks), flow_links[my_blocks]], axis=1
    )
    within = (wanted % blocks)[:, :, None] * pieces + jnp.arange(pieces, dtype=jnp.int32)
    offset = (within // sub - mine + share) % share
    table = offset * count + (wanted // blocks)[:, :, None] * sub + within % sub

    dq, dkv, dglob = attention(
        table.reshape(-1).astype(jnp.int32),
        stats,
        pairs.reshape(count, tile, 2 * HD),
        kv,
        glob_now,
    )
    dq_back = exchange(dq.reshape(size, part, HD))
    dkv = dkv.reshape(share, size, part, 2 * HD)
    dkv_sum = dkv[0].astype(jnp.float32)
    for step in range(1, share):
        dkv_sum = dkv_sum + to_mate(dkv[step], step, share).astype(jnp.float32)
    dkv_back = exchange(dkv_sum.astype(jnp.bfloat16))
    glob_parts = lax.all_gather(dglob, "seq", axis=0, tiled=False)
    glob_sum = jnp.sum(glob_parts.reshape(heads, share, G, 2, HD), axis=1)
    glob_grads = jnp.transpose(glob_sum, (2, 1, 0, 3)).reshape(2, G, features).astype(jnp.bfloat16)

    (grad_queries,) = unpair_heads(dq_back, share)
    grad_keys, grad_values = unpair_heads(dkv_back, share)
    return (grad_queries, grad_keys, grad_values, glob_grads[0], glob_grads[1])


CHUNKS = ((0, 6), (6, 2))
UNROLL = (2, 4)
VMEM_LIMIT = 60 * 1024 * 1024


def pad_of(some):
    return (2 * some + 7) // 8 * 8


def split_two(row):
    high = row.astype(jnp.bfloat16).astype(jnp.float32)
    return jnp.concatenate([high, row - high], axis=1)


def pack_kernel(query_ref, grad_ref, saved_ref, norm_ref, out_ref):
    rows = query_ref.shape[0]
    for head in range(out_ref.shape[1]):
        cols = slice(head * HD, (head + 1) * HD)
        query = query_ref[:, cols]
        grad = grad_ref[:, cols]
        product = grad.astype(jnp.float32) * saved_ref[:, cols].astype(jnp.float32)
        delta = jnp.sum(product.T, axis=0, keepdims=True)
        norm = norm_ref[head : head + 1, :]
        stats = []
        for block in range(rows // BLK):
            lanes = slice(block * BLK, (block + 1) * BLK)
            stats += [split_two(norm[:, lanes]), split_two(delta[:, lanes])]
        pad = out_ref.shape[2] - rows
        if len(stats) < pad:
            stats.append(jnp.zeros((pad - len(stats), 2 * HD), jnp.float32))
        stats = jnp.concatenate(stats, axis=0).astype(jnp.bfloat16)
        for half in range(2):
            out_ref[half, head, :rows, :HD] = query
            out_ref[half, head, :rows, HD:] = grad
            out_ref[half, head, rows:, :] = stats


def pack_queries(queries, grad_output, saved_output, log_norm, first, some):
    tokens, features = queries.shape
    heads = features // HD
    rows = some * BLK
    place = first // some
    spec = pl.BlockSpec((rows, features), lambda i: (place, 0))
    shape = (2, heads, rows + pad_of(some), 2 * HD)
    out = pl.pallas_call(
        pack_kernel,
        grid=(1,),
        in_specs=[spec] * 3 + [pl.BlockSpec((heads, rows), lambda i: (0, place))],
        out_specs=pl.BlockSpec(shape, lambda i: (0, 0, 0, 0)),
        out_shape=jax.ShapeDtypeStruct(shape, jnp.bfloat16),
        compiler_params=pltpu.CompilerParams(vmem_limit_bytes=VMEM_LIMIT),
        cost_estimate=pl.CostEstimate(
            flops=0, bytes_accessed=rows * features * 14, transcendentals=0
        ),
    )(queries, grad_output, saved_output, log_norm)
    return out.reshape(2 * heads, rows + pad_of(some), 2 * HD)


def pack_keys_kernel(mine_ref, key_ref, value_ref, glob_key_ref, glob_value_ref, *out_refs):
    tokens = key_ref.shape[0]
    chips = len(out_refs)
    chip, core = mine_ref[0] // 2, mine_ref[0] % 2
    for step, out_ref in enumerate(out_refs):
        there = lax.rem(chip + step, chips)
        for side in range(2):
            head = 2 * there + (core if side == 0 else 1 - core)
            cols = pl.ds(pl.multiple_of(head * HD, HD), HD)
            start = side * (tokens + G)
            out_ref[start : start + tokens, :HD] = key_ref[:, cols]
            out_ref[start : start + tokens, HD:] = value_ref[:, cols]
            out_ref[start + tokens : start + tokens + G, :HD] = glob_key_ref[:, cols]
            out_ref[start + tokens : start + tokens + G, HD:] = glob_value_ref[:, cols]


def pack_keys(mine, keys, values, glob_keys, glob_values):
    tokens, features = keys.shape
    chips = features // HD // 2
    vmem = pl.BlockSpec(memory_space=pltpu.VMEM)
    return pl.pallas_call(
        pack_keys_kernel,
        in_specs=[pl.BlockSpec(memory_space=pltpu.SMEM)] + [vmem] * 4,
        out_specs=[vmem] * chips,
        out_shape=[jax.ShapeDtypeStruct((2 * (tokens + G), 2 * HD), jnp.bfloat16)] * chips,
        compiler_params=pltpu.CompilerParams(vmem_limit_bytes=VMEM_LIMIT),
        cost_estimate=pl.CostEstimate(
            flops=0, bytes_accessed=(tokens + G) * features * 8, transcendentals=0
        ),
    )(mine, keys, values, glob_keys, glob_values)


def pair_grads(pair, stats, rows, valid):
    zero = jnp.zeros((BLK, HD), jnp.bfloat16)
    mixed = jnp.concatenate(
        [
            jnp.concatenate([pair[:, :HD], zero], axis=1),
            jnp.concatenate([zero, pair[:, HD:]], axis=1),
        ],
        axis=0,
    )
    norm = (stats[0:1, :HD] + stats[0:1, HD:]) * LOG2E
    delta = stats[1:2, :HD] + stats[1:2, HD:]
    rows = jnp.concatenate(rows, axis=0) if len(rows) > 1 else rows[0]
    both = lax.dot_general(
        rows, mixed, (((1,), (1,)), ((), ())), preferred_element_type=jnp.float32
    )
    attend = jnp.exp2(both[:, :HD] * (FACTOR * LOG2E) - norm)
    parts = []
    for kind, known in enumerate(valid):
        part = attend[kind * BLK : (kind + 1) * BLK]
        parts.append(part if known is None else jnp.where(known, part, 0.0))
    attend = jnp.concatenate(parts, axis=0) if len(parts) > 1 else parts[0]
    grad_scores = attend * (both[:, HD:] - delta)
    scores_low = grad_scores.astype(jnp.bfloat16)
    grad_kv = jnp.dot(
        jnp.concatenate([scores_low, attend.astype(jnp.bfloat16)], axis=1),
        mixed,
        preferred_element_type=jnp.float32,
    )
    grad_q = lax.dot_general(
        scores_low, rows[:, :HD], (((0,), (0,)), ((), ())), preferred_element_type=jnp.float32
    )
    return grad_kv, grad_q * FACTOR


def chunk_kernel(chunk, heads, table_ref, glob_ref, pair_ref, *refs):
    kv_refs, refs = refs[:heads], refs[heads:]
    last = chunk == len(CHUNKS) - 1
    some = CHUNKS[chunk][1]
    if last:
        before_ref, glob_before_ref, dq_ref = refs[:3]
        out_refs, refs = refs[3 : 3 + heads // 2], refs[3 + heads // 2 :]
        dglob_ref, kv, pairs, acc, sems, before, stage, out_sems = refs
    else:
        dq_ref, sum_ref, dglob_ref, kv, pairs, acc, sems = refs
    sources = pairs.shape[0]
    total = acc.shape[0]
    blocks = total // heads
    own_kinds = W + R
    own_base = heads * some * own_kinds
    rim_base = own_base + heads * some * R
    half = table_ref[rim_base + 2]
    copies = [
        pltpu.make_async_copy(
            kv_ref.at[pl.ds(step % 2 * (blocks * BLK + G), blocks * BLK), :],
            kv.at[step],
            sems.at[step],
        )
        for step, kv_ref in enumerate(kv_refs)
    ]
    copies.append(pltpu.make_async_copy(pair_ref, pairs, sems.at[heads]))
    for copy in copies:
        copy.start()
    if last:
        earlier = pltpu.make_async_copy(before_ref, before, sems.at[heads + 1])
        earlier.start()
        dglob_ref[...] = glob_before_ref[...]
    else:
        dglob_ref[...] = jnp.zeros_like(dglob_ref)

    def clear(block, carry):
        acc[block] = jnp.zeros((BLK, 2 * HD), jnp.float32)
        return carry

    lax.fori_loop(0, total, clear, 0)
    for copy in copies:
        copy.wait()

    def meet(source, inner, wanted, with_glob):
        lines = slice(inner * BLK, (inner + 1) * BLK)
        stats = pairs[source, some * BLK :, :].astype(jnp.float32)
        places = [jnp.maximum(place, 0) for place in wanted]
        rows = [
            kv[place // blocks, pl.ds(pl.multiple_of((place % blocks) * BLK, BLK), BLK), :]
            for place in places
        ]
        valid = [place >= 0 for place in wanted]
        if with_glob:
            rows.append(glob_ref[...])
            valid.append(None)
        grad_kv, grad_q = pair_grads(
            pairs[source, lines, :], stats[2 * inner : 2 * inner + 2], rows, valid
        )
        for kind, place in enumerate(places):
            acc[place] += grad_kv[kind * BLK : (kind + 1) * BLK]
        if with_glob:
            dglob_ref[...] += grad_kv[len(places) * BLK :]
        return lines, grad_q

    def one_own(index, carry):
        source = half * heads + index
        for inner in range(some):
            entry = (index * some + inner) * own_kinds
            wanted = [table_ref[entry + kind] for kind in range(own_kinds)]
            lines, grad_q = meet(source, inner, wanted, True)
            dq_ref[source, lines, :] = grad_q.astype(jnp.bfloat16)
        return carry

    def one_other(index, carry):
        source = (1 - half) * heads + index
        for inner in range(some):
            entry = own_base + (index * some + inner) * R
            wanted = [table_ref[entry + kind] for kind in range(R)]
            lines, grad_q = meet(source, inner, wanted, True)
            dq_ref[source, lines, :] = grad_q.astype(jnp.bfloat16)
        return carry

    lax.fori_loop(0, heads, one_own, 0, unroll=UNROLL[chunk])
    lax.fori_loop(0, heads, one_other, 0, unroll=UNROLL[chunk])
    rims = []
    if chunk == 0:
        rims.append((0, 0, rim_base))
    if last:
        rims.append((heads - 1, some - 1, rim_base + 1))
    for index, inner, entry in rims:
        source = (1 - half) * heads + index
        lines, grad_q = meet(source, inner, [table_ref[entry]], False)
        dq_ref[source, lines, :] = (
            dq_ref[source, lines, :].astype(jnp.float32) + grad_q
        ).astype(jnp.bfloat16)
    if not last:
        leave = pltpu.make_async_copy(acc, sum_ref, sems.at[heads + 1])
        leave.start()
        leave.wait()
        return
    dglob_ref[:, :HD] = dglob_ref[:, :HD] * FACTOR
    earlier.wait()

    def copy_out(step):
        slot = step % 2
        out = out_refs[step // 2].at[pl.ds(step % 2 * (blocks * BLK), blocks * BLK), :]
        return pltpu.make_async_copy(stage.at[slot], out, out_sems.at[slot])

    for step in range(heads):
        if step >= 2:
            copy_out(step - 2).wait()
        for inner in range(blocks):
            value = acc[step * blocks + inner] + before[step * blocks + inner]
            lines = slice(inner * BLK, (inner + 1) * BLK)
            stage[step % 2, lines, :HD] = (value[:, :HD] * FACTOR).astype(jnp.bfloat16)
            stage[step % 2, lines, HD:] = value[:, HD:].astype(jnp.bfloat16)
        copy_out(step).start()
    for step in range(max(0, heads - 2), heads):
        copy_out(step).wait()


def chunk_call(chunk, table, glob, pairs, kv, before=()):
    sources = pairs.shape[0]
    heads = len(kv)
    rows = CHUNKS[chunk][1] * BLK
    tokens = kv[0].shape[0] // 2 - G
    total = heads * (tokens // BLK)
    last = chunk == len(CHUNKS) - 1
    vmem = pl.BlockSpec(memory_space=pltpu.VMEM)
    smem = pl.BlockSpec(memory_space=pltpu.SMEM)
    hbm = pl.BlockSpec(memory_space=pl.ANY)
    sums = jax.ShapeDtypeStruct((total, BLK, 2 * HD), jnp.float32)
    rounded = jax.ShapeDtypeStruct((2 * tokens, 2 * HD), jnp.bfloat16)
    scratch = [
        pltpu.VMEM((heads, tokens, 2 * HD), jnp.bfloat16),
        pltpu.VMEM(pairs.shape, jnp.bfloat16),
        pltpu.VMEM(sums.shape, jnp.float32),
        pltpu.SemaphoreType.DMA((heads + 2,)),
    ]
    if last:
        scratch += [
            pltpu.VMEM(sums.shape, jnp.float32),
            pltpu.VMEM((2, tokens, 2 * HD), jnp.bfloat16),
            pltpu.SemaphoreType.DMA((2,)),
        ]
    units = heads * (rows // BLK) * (W + 2 * R + 2)
    return pl.pallas_call(
        functools.partial(chunk_kernel, chunk, heads),
        in_specs=[smem, vmem, hbm] + [hbm] * heads + [hbm, vmem] * last,
        out_specs=[vmem] + [hbm] * (heads // 2 if last else 1) + [vmem],
        out_shape=[jax.ShapeDtypeStruct((sources, rows, HD), jnp.bfloat16)]
        + ([rounded] * (heads // 2) if last else [sums])
        + [jax.ShapeDtypeStruct((G, 2 * HD), jnp.float32)],
        scratch_shapes=scratch,
        compiler_params=pltpu.CompilerParams(vmem_limit_bytes=VMEM_LIMIT),
        cost_estimate=pl.CostEstimate(
            flops=units * 16 * BLK * BLK * HD,
            bytes_accessed=total * BLK * HD * 16,
            transcendentals=units * BLK * BLK,
        ),
    )(table, glob, pairs, *kv, *before)


def unpack_queries_kernel(*refs):
    *in_refs, out_ref = refs
    heads = in_refs[0].shape[0] // 2
    for (first, some), in_ref in zip(CHUNKS, in_refs):
        for head in range(heads):
            total = in_ref[head].astype(jnp.float32) + in_ref[heads + head].astype(jnp.float32)
            out_ref[first * BLK : (first + some) * BLK, head * HD : (head + 1) * HD] = total.astype(
                jnp.bfloat16
            )


def unpack_queries(arrays):
    shape = (sum(array.shape[1] for array in arrays), arrays[0].shape[0] // 2 * HD)
    vmem = pl.BlockSpec(memory_space=pltpu.VMEM)
    return pl.pallas_call(
        unpack_queries_kernel,
        in_specs=[vmem] * len(arrays),
        out_specs=vmem,
        out_shape=jax.ShapeDtypeStruct(shape, jnp.bfloat16),
        compiler_params=pltpu.CompilerParams(vmem_limit_bytes=VMEM_LIMIT),
        cost_estimate=pl.CostEstimate(
            flops=0, bytes_accessed=shape[0] * shape[1] * 6, transcendentals=0
        ),
    )(*arrays)


def unpack_keys_kernel(mine_ref, *refs):
    *in_refs, dk_ref, dv_ref = refs
    chips = len(in_refs) // 2
    chip, core = mine_ref[0] // 2, mine_ref[0] % 2
    for step, in_ref in enumerate(in_refs):
        there = lax.rem(chip + step // 2, chips)
        head = 2 * there + (core if step % 2 == 0 else 1 - core)
        cols = pl.ds(pl.multiple_of(head * HD, HD), HD)
        dk_ref[:, cols] = in_ref[:, :HD]
        dv_ref[:, cols] = in_ref[:, HD:]


def unpack_keys(mine, arrays):
    tokens = arrays[0].shape[0] // 2
    heads = len(arrays)
    rows = tokens // 2
    shape = jax.ShapeDtypeStruct((tokens, heads * HD), jnp.bfloat16)
    sides = [
        pl.BlockSpec((rows, 2 * HD), lambda i: (i, 0)),
        pl.BlockSpec((rows, 2 * HD), lambda i: (2 + i, 0)),
    ]
    return pl.pallas_call(
        unpack_keys_kernel,
        grid=(2,),
        in_specs=[pl.BlockSpec(memory_space=pltpu.SMEM)] + sides * (heads // 2),
        out_specs=[pl.BlockSpec((rows, heads * HD), lambda i: (i, 0))] * 2,
        out_shape=[shape] * 2,
        compiler_params=pltpu.CompilerParams(vmem_limit_bytes=VMEM_LIMIT),
        cost_estimate=pl.CostEstimate(
            flops=0, bytes_accessed=tokens * heads * HD * 8, transcendentals=0
        ),
    )(mine, *arrays)


def body_halves(
    queries,
    keys,
    values,
    saved_output,
    grad_output,
    log_norm,
    global_keys,
    global_values,
    flow_links,
    glob_owner,
):
    size = lax.axis_size("seq")
    my_index = lax.axis_index("seq")
    tokens, features = queries.shape
    heads = features // HD
    blocks = tokens // BLK
    count = heads * blocks
    half = my_index // heads
    mine = my_index % heads
    mine_one = mine.astype(jnp.int32).reshape(1)

    chips = heads // 2

    def turn(array, step):
        pairs = [
            (i, i - i % heads + (i % heads // 2 + step) % chips * 2 + i % 2) for i in range(size)
        ]
        return lax.ppermute(array, "seq", pairs) if step % chips else array

    def over(array):
        return lax.ppermute(array, "seq", [(i, i ^ 1) for i in range(size)])

    first = exchange(pack_queries(queries, grad_output, saved_output, log_norm, *CHUNKS[0]))
    owned = (glob_owner == my_index)[:, None]
    (*slabs,) = pack_keys(
        mine_one,
        keys,
        values,
        jnp.where(owned, global_keys[0], jnp.bfloat16(0)),
        jnp.where(owned, global_values[0], jnp.bfloat16(0)),
    )
    packed = pack_queries(queries, grad_output, saved_output, log_norm, *CHUNKS[1])
    slabs[3], packed = lax.optimization_barrier((slabs[3], packed))
    near_kv = [turn(slab, step) for step, slab in enumerate(slabs)]
    kv = [piece for slab in near_kv for piece in (slab, over(slab))]
    packed, first, kv[4] = lax.optimization_barrier((packed, first, kv[4]))
    second = exchange(packed)
    glob_now = functools.reduce(
        jnp.add,
        [
            piece[tokens + step % 2 * (tokens + G) :][:G].astype(jnp.float32)
            for step, piece in enumerate(kv)
        ],
    ).astype(jnp.bfloat16)

    def places(wanted):
        here = wanted - half * count
        owner = here // blocks
        step = (mine // 2 - owner // 2 + chips) % chips * 2 + (mine + owner) % 2
        return jnp.where((here >= 0) & (here < count), step * blocks + here % blocks, -1)

    links = flow_links.reshape(2, count, R)
    my_links = lax.dynamic_index_in_dim(links, half, axis=0, keepdims=False)
    other_links = lax.dynamic_index_in_dim(links, 1 - half, axis=0, keepdims=False)
    order = half * count + jnp.arange(count, dtype=jnp.int32)
    near = (order[:, None] + jnp.arange(-1, 2, dtype=jnp.int32) + 2 * count) % (2 * count)
    own = places(jnp.concatenate([near, my_links], axis=1)).reshape(heads, blocks, -1)
    other = places(other_links).reshape(heads, blocks, -1)
    ends = places(jnp.stack([half * count + count - 1, half * count]))
    tail = jnp.concatenate([ends, half.reshape(1)])
    tables = [
        jnp.concatenate(
            [part[:, first : first + some].reshape(-1) for part in (own, other)] + [tail]
        ).astype(jnp.int32)
        for first, some in CHUNKS
    ]

    dq_first, sums, dglob = chunk_call(0, tables[0], glob_now, first, kv)
    back_first = exchange(dq_first)
    dq_second, *slabs, dglob = chunk_call(1, tables[1], glob_now, second, kv, (sums, dglob))
    dq_second, back_first = lax.optimization_barrier((dq_second, back_first))
    slabs = [turn(slab, chips - step) for step, slab in enumerate(slabs)]
    dq_second, slabs[2] = lax.optimization_barrier((dq_second, slabs[2]))
    back_second = exchange(dq_second)
    grad_keys, grad_values = unpack_keys(
        mine_one, [piece for slab in slabs for piece in (slab, over(slab))]
    )
    grad_queries = unpack_queries((back_first, back_second))
    held = (glob_owner // heads == half)[:, None]
    glob_parts = lax.all_gather(
        jnp.where(held, dglob, 0.0).astype(jnp.bfloat16), "seq", axis=0, tiled=False
    ).astype(jnp.float32)
    glob_sum = (glob_parts[:heads] + glob_parts[heads:]).reshape(heads, G, 2, HD)
    glob_grads = jnp.transpose(glob_sum, (2, 1, 0, 3)).reshape(2, G, features).astype(jnp.bfloat16)
    return (grad_queries, grad_keys, grad_values, glob_grads[0], glob_grads[1])


def body(queries, *rest):
    tokens, features = queries.shape
    blocks = sum(some for _, some in CHUNKS)
    if lax.axis_size("seq") == 2 * (features // HD) and tokens == blocks * BLK:
        return body_halves(queries, *rest)
    return body_shared(queries, *rest)


def solution(mesh):
    return jax.shard_map(
        body,
        mesh=mesh,
        in_specs=(
            P("seq", "tp"),
            P("seq", "tp"),
            P("seq", "tp"),
            P("seq", "tp"),
            P("seq", "tp"),
            P("tp", "seq"),
            P("seq", None, "tp"),
            P("seq", None, "tp"),
            P(),
            P(),
        ),
        out_specs=(P("seq", "tp"), P("seq", "tp"), P("seq", "tp"), P(None, "tp"), P(None, "tp")),
        check_vma=False,
    )
```

```python
import functools
import math

import jax
import jax.numpy as jnp
from jax import lax
from jax.experimental import pallas as pl
from jax.experimental.pallas import tpu as pltpu
from jax.sharding import PartitionSpec as P

HD = 128
BLK = 128
R = 3
G = 128
W = 3
FACTOR = HD ** (-0.5)
LOG2E = math.log2(math.e)
STAGE = 4


def pair_kernel(left_ref, right_ref, out_ref):
    heads = out_ref.shape[0]
    for head in range(heads):
        cols = slice(head * HD, (head + 1) * HD)
        out_ref[head, 0, :, :HD] = left_ref[:, cols]
        out_ref[head, 0, :, HD:] = right_ref[:, cols]


def pair_heads(left, right, share):
    tokens, features = left.shape
    heads = features // HD
    part = tokens // share
    rows = min(256, part)
    steps = part // rows
    out = pl.pallas_call(
        pair_kernel,
        grid=(share, steps),
        in_specs=[pl.BlockSpec((rows, features), lambda s, t: (s * steps + t, 0))] * 2,
        out_specs=pl.BlockSpec((heads, 1, rows, 2 * HD), lambda s, t: (0, s, t, 0)),
        out_shape=jax.ShapeDtypeStruct((heads, share, part, 2 * HD), left.dtype),
        cost_estimate=pl.CostEstimate(
            flops=0, bytes_accessed=4 * tokens * features * 2, transcendentals=0
        ),
    )(left, right)
    return out.reshape(heads * share, part, 2 * HD)


def unpair_kernel(in_ref, *out_refs):
    heads = in_ref.shape[0]
    for head in range(heads):
        cols = slice(head * HD, (head + 1) * HD)
        for which, out_ref in enumerate(out_refs):
            out_ref[:, cols] = in_ref[head, 0, :, which * HD : (which + 1) * HD]


def unpair_heads(mixed, share):
    parts, part, width = mixed.shape
    heads = parts // share
    count = width // HD
    rows = min(256, part)
    steps = part // rows
    shape = jax.ShapeDtypeStruct((share * part, heads * HD), mixed.dtype)
    return pl.pallas_call(
        unpair_kernel,
        grid=(share, steps),
        in_specs=[pl.BlockSpec((heads, 1, rows, width), lambda s, t: (0, s, t, 0))],
        out_specs=[pl.BlockSpec((rows, heads * HD), lambda s, t: (s * steps + t, 0))] * count,
        out_shape=[shape] * count,
        cost_estimate=pl.CostEstimate(
            flops=0, bytes_accessed=4 * parts * part * width, transcendentals=0
        ),
    )(mixed.reshape(heads, share, part, width))


def attention_kernel(
    table_ref, stats_ref, pair_ref, kv_ref, glob_ref, dq_ref, dkv_ref, dglob_ref, acc, stage, sems
):
    count, tile, _ = pair_ref.shape
    total = acc.shape[0]
    kinds = (W + R) * (BLK // tile)

    def clear(block, carry):
        acc[block] = jnp.zeros((tile, 2 * HD), jnp.float32)
        return carry

    lax.fori_loop(0, total, clear, 0)
    dglob_ref[...] = jnp.zeros_like(dglob_ref)
    zero = jnp.zeros((tile, HD), jnp.bfloat16)

    def one_block(block, carry):
        pair = pair_ref[block]
        mixed = jnp.concatenate(
            [
                jnp.concatenate([pair[:, :HD], zero], axis=1),
                jnp.concatenate([zero, pair[:, HD:]], axis=1),
            ],
            axis=0,
        )
        stats = stats_ref[block]
        norm = stats[0:1] * LOG2E
        delta = stats[1:2]
        places = [table_ref[block * kinds + kind] for kind in range(kinds)]
        rows = jnp.concatenate([kv_ref[place] for place in places] + [glob_ref[...]], axis=0)
        both = lax.dot_general(
            rows, mixed, (((1,), (1,)), ((), ())), preferred_element_type=jnp.float32
        )
        attend = jnp.exp2(both[:, :tile] * (FACTOR * LOG2E) - norm)
        grad_scores = attend * (both[:, tile:] - delta)
        attend_low = attend.astype(jnp.bfloat16)
        scores_low = grad_scores.astype(jnp.bfloat16)
        grad_kv = jnp.dot(
            jnp.concatenate([scores_low, attend_low], axis=1),
            mixed,
            preferred_element_type=jnp.float32,
        )
        for kind, place in enumerate(places):
            acc[place] += grad_kv[kind * tile : (kind + 1) * tile]
        dglob_ref[...] += grad_kv[kinds * tile :]
        grad_q = lax.dot_general(
            scores_low, rows[:, :HD], (((0,), (0,)), ((), ())), preferred_element_type=jnp.float32
        )
        dq_ref[block] = (grad_q * FACTOR).astype(jnp.bfloat16)
        return carry

    lax.fori_loop(0, count, one_block, 0)
    dglob_ref[:, :HD] = dglob_ref[:, :HD] * FACTOR

    def copy_out(step, slot):
        return pltpu.make_async_copy(
            stage.at[slot], dkv_ref.at[pl.ds(step * STAGE, STAGE)], sems.at[slot]
        )

    steps = total // STAGE
    for step in range(steps):
        slot = step % 2
        if step >= 2:
            copy_out(step - 2, slot).wait()
        part = acc[step * STAGE : (step + 1) * STAGE]
        stage[slot, :, :, :HD] = (part[:, :, :HD] * FACTOR).astype(jnp.bfloat16)
        stage[slot, :, :, HD:] = part[:, :, HD:].astype(jnp.bfloat16)
        copy_out(step, slot).start()
    for step in range(max(0, steps - 2), steps):
        copy_out(step, step % 2).wait()


def attention(table, stats, pairs, kv, glob):
    count, tile, _ = pairs.shape
    total = kv.shape[0]
    vmem = pl.BlockSpec(memory_space=pltpu.VMEM)
    return pl.pallas_call(
        attention_kernel,
        in_specs=[pl.BlockSpec(memory_space=pltpu.SMEM), vmem, vmem, vmem, vmem],
        out_specs=[vmem, pl.BlockSpec(memory_space=pl.ANY), vmem],
        out_shape=[
            jax.ShapeDtypeStruct((count, tile, HD), jnp.bfloat16),
            jax.ShapeDtypeStruct((total, tile, 2 * HD), jnp.bfloat16),
            jax.ShapeDtypeStruct((G, 2 * HD), jnp.float32),
        ],
        scratch_shapes=[
            pltpu.VMEM((total, tile, 2 * HD), jnp.float32),
            pltpu.VMEM((2, STAGE, tile, 2 * HD), jnp.bfloat16),
            pltpu.SemaphoreType.DMA((2,)),
        ],
        compiler_params=pltpu.CompilerParams(vmem_limit_bytes=60 * 1024 * 1024),
        cost_estimate=pl.CostEstimate(
            flops=count * (W + R + 1) * 10 * tile * BLK * HD,
            bytes_accessed=(total * 8 + count * 6) * tile * HD,
            transcendentals=count * (W + R + 1) * tile * BLK,
        ),
    )(table, stats, pairs, kv, glob)


def exchange(array):
    return lax.all_to_all(array, "seq", split_axis=0, concat_axis=0, tiled=True)


def to_mate(array, step, share):
    size = lax.axis_size("seq")
    return lax.ppermute(
        array, "seq", [(i, i - i % share + (i + step) % share) for i in range(size)]
    )


def body_shared(
    queries,
    keys,
    values,
    saved_output,
    grad_output,
    log_norm,
    global_keys,
    global_values,
    flow_links,
    glob_owner,
):
    size = lax.axis_size("seq")
    tokens, features = queries.shape
    heads = features // HD
    blocks = tokens // BLK
    share = size // heads
    part = tokens // share
    tile = min(BLK, part)
    sub = part // tile
    pieces = BLK // tile
    count = size * sub
    mine = lax.axis_index("seq") % share

    kv_own = exchange(pair_heads(keys, values, share))
    glob_pair = jnp.concatenate(
        [global_keys.reshape(G, heads, HD), global_values.reshape(G, heads, HD)], axis=2
    )
    glob_out = jnp.repeat(jnp.transpose(glob_pair, (1, 0, 2)), share, axis=0)
    glob_in = exchange(glob_out)
    product = grad_output.astype(jnp.float32) * saved_output.astype(jnp.float32)
    delta = jnp.sum(product.reshape(tokens, heads, HD), axis=2).T
    stats_out = jnp.stack(
        [log_norm.reshape(size, part), delta.reshape(size, part)], axis=1
    )
    stats_in = exchange(stats_out)
    pairs = exchange(pair_heads(queries, grad_output, share))

    owners = jnp.arange(size, dtype=jnp.int32)[:, None] == glob_owner[None, :]
    glob_now = jnp.sum(
        jnp.where(owners[:, :, None], glob_in.astype(jnp.float32), 0.0), axis=0
    ).astype(jnp.bfloat16)
    stats = jnp.transpose(stats_in.reshape(size, 2, sub, tile), (0, 2, 1, 3)).reshape(
        count, 2, tile
    )
    kv = jnp.concatenate(
        [kv_own] + [to_mate(kv_own, share - step, share) for step in range(1, share)], axis=0
    ).reshape(share * count, tile, 2 * HD)

    order = jnp.arange(count, dtype=jnp.int32)
    my_blocks = (order // sub) * blocks + (mine * sub + order % sub) // pieces
    near = my_blocks[:, None] + jnp.arange(-1, 2, dtype=jnp.int32)[None, :]
    wanted = jnp.concatenate(
        [(near + size * blocks) % (size * blocks), flow_links[my_blocks]], axis=1
    )
    within = (wanted % blocks)[:, :, None] * pieces + jnp.arange(pieces, dtype=jnp.int32)
    offset = (within // sub - mine + share) % share
    table = offset * count + (wanted // blocks)[:, :, None] * sub + within % sub

    dq, dkv, dglob = attention(
        table.reshape(-1).astype(jnp.int32),
        stats,
        pairs.reshape(count, tile, 2 * HD),
        kv,
        glob_now,
    )
    dq_back = exchange(dq.reshape(size, part, HD))
    dkv = dkv.reshape(share, size, part, 2 * HD)
    dkv_sum = dkv[0].astype(jnp.float32)
    for step in range(1, share):
        dkv_sum = dkv_sum + to_mate(dkv[step], step, share).astype(jnp.float32)
    dkv_back = exchange(dkv_sum.astype(jnp.bfloat16))
    glob_parts = lax.all_gather(dglob, "seq", axis=0, tiled=False)
    glob_sum = jnp.sum(glob_parts.reshape(heads, share, G, 2, HD), axis=1)
    glob_grads = jnp.transpose(glob_sum, (2, 1, 0, 3)).reshape(2, G, features).astype(jnp.bfloat16)

    (grad_queries,) = unpair_heads(dq_back, share)
    grad_keys, grad_values = unpair_heads(dkv_back, share)
    return (grad_queries, grad_keys, grad_values, glob_grads[0], glob_grads[1])


CHUNKS = ((0, 6), (6, 2))
UNROLL = (2, 4)
VMEM_LIMIT = 60 * 1024 * 1024


def pad_of(some):
    return (2 * some + 7) // 8 * 8


def split_two(row):
    high = row.astype(jnp.bfloat16).astype(jnp.float32)
    return jnp.concatenate([high, row - high], axis=1)


def pack_kernel(query_ref, grad_ref, saved_ref, norm_ref, out_ref):
    rows = query_ref.shape[0]
    for head in range(out_ref.shape[1]):
        cols = slice(head * HD, (head + 1) * HD)
        query = query_ref[:, cols]
        grad = grad_ref[:, cols]
        product = grad.astype(jnp.float32) * saved_ref[:, cols].astype(jnp.float32)
        delta = jnp.sum(product.T, axis=0, keepdims=True)
        norm = norm_ref[head : head + 1, :]
        stats = []
        for block in range(rows // BLK):
            lanes = slice(block * BLK, (block + 1) * BLK)
            stats += [split_two(norm[:, lanes]), split_two(delta[:, lanes])]
        pad = out_ref.shape[2] - rows
        if len(stats) < pad:
            stats.append(jnp.zeros((pad - len(stats), 2 * HD), jnp.float32))
        stats = jnp.concatenate(stats, axis=0).astype(jnp.bfloat16)
        for half in range(2):
            out_ref[half, head, :rows, :HD] = query
            out_ref[half, head, :rows, HD:] = grad
            out_ref[half, head, rows:, :] = stats


def pack_queries(queries, grad_output, saved_output, log_norm, first, some):
    tokens, features = queries.shape
    heads = features // HD
    rows = some * BLK
    place = first // some
    spec = pl.BlockSpec((rows, features), lambda i: (place, 0))
    shape = (2, heads, rows + pad_of(some), 2 * HD)
    out = pl.pallas_call(
        pack_kernel,
        grid=(1,),
        in_specs=[spec] * 3 + [pl.BlockSpec((heads, rows), lambda i: (0, place))],
        out_specs=pl.BlockSpec(shape, lambda i: (0, 0, 0, 0)),
        out_shape=jax.ShapeDtypeStruct(shape, jnp.bfloat16),
        compiler_params=pltpu.CompilerParams(vmem_limit_bytes=VMEM_LIMIT),
        cost_estimate=pl.CostEstimate(
            flops=0, bytes_accessed=rows * features * 14, transcendentals=0
        ),
    )(queries, grad_output, saved_output, log_norm)
    return out.reshape(2 * heads, rows + pad_of(some), 2 * HD)


def pack_keys_kernel(mine_ref, key_ref, value_ref, glob_key_ref, glob_value_ref, *out_refs):
    tokens = key_ref.shape[0]
    chips = len(out_refs)
    chip, core = mine_ref[0] // 2, mine_ref[0] % 2
    for step, out_ref in enumerate(out_refs):
        there = lax.rem(chip + step, chips)
        for side in range(2):
            head = 2 * there + (core if side == 0 else 1 - core)
            cols = pl.ds(pl.multiple_of(head * HD, HD), HD)
            start = side * (tokens + G)
            out_ref[start : start + tokens, :HD] = key_ref[:, cols]
            out_ref[start : start + tokens, HD:] = value_ref[:, cols]
            out_ref[start + tokens : start + tokens + G, :HD] = glob_key_ref[:, cols]
            out_ref[start + tokens : start + tokens + G, HD:] = glob_value_ref[:, cols]


def pack_keys(mine, keys, values, glob_keys, glob_values):
    tokens, features = keys.shape
    chips = features // HD // 2
    vmem = pl.BlockSpec(memory_space=pltpu.VMEM)
    return pl.pallas_call(
        pack_keys_kernel,
        in_specs=[pl.BlockSpec(memory_space=pltpu.SMEM)] + [vmem] * 4,
        out_specs=[vmem] * chips,
        out_shape=[jax.ShapeDtypeStruct((2 * (tokens + G), 2 * HD), jnp.bfloat16)] * chips,
        compiler_params=pltpu.CompilerParams(vmem_limit_bytes=VMEM_LIMIT),
        cost_estimate=pl.CostEstimate(
            flops=0, bytes_accessed=(tokens + G) * features * 8, transcendentals=0
        ),
    )(mine, keys, values, glob_keys, glob_values)


def pair_grads(pair, stats, rows, valid):
    zero = jnp.zeros((BLK, HD), jnp.bfloat16)
    mixed = jnp.concatenate(
        [
            jnp.concatenate([pair[:, :HD], zero], axis=1),
            jnp.concatenate([zero, pair[:, HD:]], axis=1),
        ],
        axis=0,
    )
    norm = (stats[0:1, :HD] + stats[0:1, HD:]) * LOG2E
    delta = stats[1:2, :HD] + stats[1:2, HD:]
    rows = jnp.concatenate(rows, axis=0) if len(rows) > 1 else rows[0]
    both = lax.dot_general(
        rows, mixed, (((1,), (1,)), ((), ())), preferred_element_type=jnp.float32
    )
    attend = jnp.exp2(both[:, :HD] * (FACTOR * LOG2E) - norm)
    parts = []
    for kind, known in enumerate(valid):
        part = attend[kind * BLK : (kind + 1) * BLK]
        parts.append(part if known is None else jnp.where(known, part, 0.0))
    attend = jnp.concatenate(parts, axis=0) if len(parts) > 1 else parts[0]
    grad_scores = attend * (both[:, HD:] - delta)
    scores_low = grad_scores.astype(jnp.bfloat16)
    grad_kv = jnp.dot(
        jnp.concatenate([scores_low, attend.astype(jnp.bfloat16)], axis=1),
        mixed,
        preferred_element_type=jnp.float32,
    )
    grad_q = lax.dot_general(
        scores_low, rows[:, :HD], (((0,), (0,)), ((), ())), preferred_element_type=jnp.float32
    )
    return grad_kv, grad_q * FACTOR


def chunk_kernel(chunk, heads, table_ref, glob_ref, pair_ref, *refs):
    kv_refs, refs = refs[:heads], refs[heads:]
    last = chunk == len(CHUNKS) - 1
    some = CHUNKS[chunk][1]
    if last:
        before_ref, glob_before_ref, dq_ref = refs[:3]
        out_refs, refs = refs[3 : 3 + heads // 2], refs[3 + heads // 2 :]
        dglob_ref, kv, pairs, acc, sems, before, stage, out_sems = refs
    else:
        dq_ref, sum_ref, dglob_ref, kv, pairs, acc, sems = refs
    sources = pairs.shape[0]
    total = acc.shape[0]
    blocks = total // heads
    own_kinds = W + R
    own_base = heads * some * own_kinds
    rim_base = own_base + heads * some * R
    half = table_ref[rim_base + 2]
    copies = [
        pltpu.make_async_copy(
            kv_ref.at[pl.ds(step % 2 * (blocks * BLK + G), blocks * BLK), :],
            kv.at[step],
            sems.at[step],
        )
        for step, kv_ref in enumerate(kv_refs)
    ]
    copies.append(pltpu.make_async_copy(pair_ref, pairs, sems.at[heads]))
    for copy in copies:
        copy.start()
    if last:
        earlier = pltpu.make_async_copy(before_ref, before, sems.at[heads + 1])
        earlier.start()
        dglob_ref[...] = glob_before_ref[...]
    else:
        dglob_ref[...] = jnp.zeros_like(dglob_ref)

    def clear(block, carry):
        acc[block] = jnp.zeros((BLK, 2 * HD), jnp.float32)
        return carry

    lax.fori_loop(0, total, clear, 0)
    for copy in copies:
        copy.wait()

    def meet(source, inner, wanted, with_glob):
        lines = slice(inner * BLK, (inner + 1) * BLK)
        stats = pairs[source, some * BLK :, :].astype(jnp.float32)
        places = [jnp.maximum(place, 0) for place in wanted]
        rows = [
            kv[place // blocks, pl.ds(pl.multiple_of((place % blocks) * BLK, BLK), BLK), :]
            for place in places
        ]
        valid = [place >= 0 for place in wanted]
        if with_glob:
            rows.append(glob_ref[...])
            valid.append(None)
        grad_kv, grad_q = pair_grads(
            pairs[source, lines, :], stats[2 * inner : 2 * inner + 2], rows, valid
        )
        for kind, place in enumerate(places):
            acc[place] += grad_kv[kind * BLK : (kind + 1) * BLK]
        if with_glob:
            dglob_ref[...] += grad_kv[len(places) * BLK :]
        return lines, grad_q

    def one_own(index, carry):
        source = half * heads + index
        for inner in range(some):
            entry = (index * some + inner) * own_kinds
            wanted = [table_ref[entry + kind] for kind in range(own_kinds)]
            lines, grad_q = meet(source, inner, wanted, True)
            dq_ref[source, lines, :] = grad_q.astype(jnp.bfloat16)
        return carry

    def one_other(index, carry):
        source = (1 - half) * heads + index
        for inner in range(some):
            entry = own_base + (index * some + inner) * R
            wanted = [table_ref[entry + kind] for kind in range(R)]
            lines, grad_q = meet(source, inner, wanted, True)
            dq_ref[source, lines, :] = grad_q.astype(jnp.bfloat16)
        return carry

    lax.fori_loop(0, heads, one_own, 0, unroll=UNROLL[chunk])
    lax.fori_loop(0, heads, one_other, 0, unroll=UNROLL[chunk])
    rims = []
    if chunk == 0:
        rims.append((0, 0, rim_base))
    if last:
        rims.append((heads - 1, some - 1, rim_base + 1))
    for index, inner, entry in rims:
        source = (1 - half) * heads + index
        lines, grad_q = meet(source, inner, [table_ref[entry]], False)
        dq_ref[source, lines, :] = (
            dq_ref[source, lines, :].astype(jnp.float32) + grad_q
        ).astype(jnp.bfloat16)
    if not last:
        leave = pltpu.make_async_copy(acc, sum_ref, sems.at[heads + 1])
        leave.start()
        leave.wait()
        return
    dglob_ref[:, :HD] = dglob_ref[:, :HD] * FACTOR
    earlier.wait()

    def copy_out(step):
        slot = step % 2
        out = out_refs[step // 2].at[pl.ds(step % 2 * (blocks * BLK), blocks * BLK), :]
        return pltpu.make_async_copy(stage.at[slot], out, out_sems.at[slot])

    for step in range(heads):
        if step >= 2:
            copy_out(step - 2).wait()
        for inner in range(blocks):
            value = acc[step * blocks + inner] + before[step * blocks + inner]
            lines = slice(inner * BLK, (inner + 1) * BLK)
            stage[step % 2, lines, :HD] = (value[:, :HD] * FACTOR).astype(jnp.bfloat16)
            stage[step % 2, lines, HD:] = value[:, HD:].astype(jnp.bfloat16)
        copy_out(step).start()
    for step in range(max(0, heads - 2), heads):
        copy_out(step).wait()


def chunk_call(chunk, table, glob, pairs, kv, before=()):
    sources = pairs.shape[0]
    heads = len(kv)
    rows = CHUNKS[chunk][1] * BLK
    tokens = kv[0].shape[0] // 2 - G
    total = heads * (tokens // BLK)
    last = chunk == len(CHUNKS) - 1
    vmem = pl.BlockSpec(memory_space=pltpu.VMEM)
    smem = pl.BlockSpec(memory_space=pltpu.SMEM)
    hbm = pl.BlockSpec(memory_space=pl.ANY)
    sums = jax.ShapeDtypeStruct((total, BLK, 2 * HD), jnp.float32)
    rounded = jax.ShapeDtypeStruct((2 * tokens, 2 * HD), jnp.bfloat16)
    scratch = [
        pltpu.VMEM((heads, tokens, 2 * HD), jnp.bfloat16),
        pltpu.VMEM(pairs.shape, jnp.bfloat16),
        pltpu.VMEM(sums.shape, jnp.float32),
        pltpu.SemaphoreType.DMA((heads + 2,)),
    ]
    if last:
        scratch += [
            pltpu.VMEM(sums.shape, jnp.float32),
            pltpu.VMEM((2, tokens, 2 * HD), jnp.bfloat16),
            pltpu.SemaphoreType.DMA((2,)),
        ]
    units = heads * (rows // BLK) * (W + 2 * R + 2)
    return pl.pallas_call(
        functools.partial(chunk_kernel, chunk, heads),
        in_specs=[smem, vmem, hbm] + [hbm] * heads + [hbm, vmem] * last,
        out_specs=[vmem] + [hbm] * (heads // 2 if last else 1) + [vmem],
        out_shape=[jax.ShapeDtypeStruct((sources, rows, HD), jnp.bfloat16)]
        + ([rounded] * (heads // 2) if last else [sums])
        + [jax.ShapeDtypeStruct((G, 2 * HD), jnp.float32)],
        scratch_shapes=scratch,
        compiler_params=pltpu.CompilerParams(vmem_limit_bytes=VMEM_LIMIT),
        cost_estimate=pl.CostEstimate(
            flops=units * 16 * BLK * BLK * HD,
            bytes_accessed=total * BLK * HD * 16,
            transcendentals=units * BLK * BLK,
        ),
    )(table, glob, pairs, *kv, *before)


def unpack_queries_kernel(in_ref, *refs):
    out_ref = refs[-1]
    heads = in_ref.shape[0] // 2
    for head in range(heads):
        total = in_ref[head].astype(jnp.float32) + in_ref[heads + head].astype(jnp.float32)
        out_ref[:, head * HD : (head + 1) * HD] = total.astype(jnp.bfloat16)


def unpack_queries(array, chunk, tokens, *before):
    first, some = CHUNKS[chunk]
    sources, rows, _ = array.shape
    width = sources // 2 * HD
    place = first // some
    return pl.pallas_call(
        unpack_queries_kernel,
        grid=(1,),
        in_specs=[pl.BlockSpec(array.shape, lambda i: (0, 0, 0))]
        + [pl.BlockSpec(memory_space=pl.ANY)] * len(before),
        out_specs=pl.BlockSpec((rows, width), lambda i: (place, 0)),
        out_shape=jax.ShapeDtypeStruct((tokens, width), jnp.bfloat16),
        input_output_aliases={1: 0} if before else {},
        compiler_params=pltpu.CompilerParams(vmem_limit_bytes=VMEM_LIMIT),
        cost_estimate=pl.CostEstimate(
            flops=0, bytes_accessed=rows * width * 6, transcendentals=0
        ),
    )(array, *before)


def unpack_keys_kernel(mine_ref, *refs):
    *in_refs, dk_ref, dv_ref = refs
    chips = len(in_refs) // 2
    chip, core = mine_ref[0] // 2, mine_ref[0] % 2
    for step, in_ref in enumerate(in_refs):
        there = lax.rem(chip + step // 2, chips)
        head = 2 * there + (core if step % 2 == 0 else 1 - core)
        cols = pl.ds(pl.multiple_of(head * HD, HD), HD)
        dk_ref[:, cols] = in_ref[:, :HD]
        dv_ref[:, cols] = in_ref[:, HD:]


def unpack_keys(mine, arrays):
    tokens = arrays[0].shape[0] // 2
    heads = len(arrays)
    rows = tokens // 2
    shape = jax.ShapeDtypeStruct((tokens, heads * HD), jnp.bfloat16)
    sides = [
        pl.BlockSpec((rows, 2 * HD), lambda i: (i, 0)),
        pl.BlockSpec((rows, 2 * HD), lambda i: (2 + i, 0)),
    ]
    return pl.pallas_call(
        unpack_keys_kernel,
        grid=(2,),
        in_specs=[pl.BlockSpec(memory_space=pltpu.SMEM)] + sides * (heads // 2),
        out_specs=[pl.BlockSpec((rows, heads * HD), lambda i: (i, 0))] * 2,
        out_shape=[shape] * 2,
        compiler_params=pltpu.CompilerParams(vmem_limit_bytes=VMEM_LIMIT),
        cost_estimate=pl.CostEstimate(
            flops=0, bytes_accessed=tokens * heads * HD * 8, transcendentals=0
        ),
    )(mine, *arrays)


def body_halves(
    queries,
    keys,
    values,
    saved_output,
    grad_output,
    log_norm,
    global_keys,
    global_values,
    flow_links,
    glob_owner,
):
    size = lax.axis_size("seq")
    my_index = lax.axis_index("seq")
    tokens, features = queries.shape
    heads = features // HD
    blocks = tokens // BLK
    count = heads * blocks
    half = my_index // heads
    mine = my_index % heads
    mine_one = mine.astype(jnp.int32).reshape(1)

    chips = heads // 2

    def turn(array, step):
        pairs = [
            (i, i - i % heads + (i % heads // 2 + step) % chips * 2 + i % 2) for i in range(size)
        ]
        return lax.ppermute(array, "seq", pairs) if step % chips else array

    def over(array):
        return lax.ppermute(array, "seq", [(i, i ^ 1) for i in range(size)])

    first = exchange(pack_queries(queries, grad_output, saved_output, log_norm, *CHUNKS[0]))
    owned = (glob_owner == my_index)[:, None]
    (*slabs,) = pack_keys(
        mine_one,
        keys,
        values,
        jnp.where(owned, global_keys[0], jnp.bfloat16(0)),
        jnp.where(owned, global_values[0], jnp.bfloat16(0)),
    )
    packed = pack_queries(queries, grad_output, saved_output, log_norm, *CHUNKS[1])
    slabs[3], packed = lax.optimization_barrier((slabs[3], packed))
    near_kv = [turn(slab, step) for step, slab in enumerate(slabs)]
    kv = [piece for slab in near_kv for piece in (slab, over(slab))]
    packed, first, kv[4] = lax.optimization_barrier((packed, first, kv[4]))
    second = exchange(packed)
    glob_now = functools.reduce(
        jnp.add,
        [
            piece[tokens + step % 2 * (tokens + G) :][:G].astype(jnp.float32)
            for step, piece in enumerate(kv)
        ],
    ).astype(jnp.bfloat16)

    def places(wanted):
        here = wanted - half * count
        owner = here // blocks
        step = (mine // 2 - owner // 2 + chips) % chips * 2 + (mine + owner) % 2
        return jnp.where((here >= 0) & (here < count), step * blocks + here % blocks, -1)

    links = flow_links.reshape(2, count, R)
    my_links = lax.dynamic_index_in_dim(links, half, axis=0, keepdims=False)
    other_links = lax.dynamic_index_in_dim(links, 1 - half, axis=0, keepdims=False)
    order = half * count + jnp.arange(count, dtype=jnp.int32)
    near = (order[:, None] + jnp.arange(-1, 2, dtype=jnp.int32) + 2 * count) % (2 * count)
    own = places(jnp.concatenate([near, my_links], axis=1)).reshape(heads, blocks, -1)
    other = places(other_links).reshape(heads, blocks, -1)
    ends = places(jnp.stack([half * count + count - 1, half * count]))
    tail = jnp.concatenate([ends, half.reshape(1)])
    tables = [
        jnp.concatenate(
            [part[:, first : first + some].reshape(-1) for part in (own, other)] + [tail]
        ).astype(jnp.int32)
        for first, some in CHUNKS
    ]

    dq_first, sums, dglob = chunk_call(0, tables[0], glob_now, first, kv)
    back_first = exchange(dq_first)
    dq_second, *slabs, dglob = chunk_call(1, tables[1], glob_now, second, kv, (sums, dglob))
    dq_second, back_first = lax.optimization_barrier((dq_second, back_first))
    slabs = [turn(slab, chips - step) for step, slab in enumerate(slabs)]
    dq_second, slabs[2] = lax.optimization_barrier((dq_second, slabs[2]))
    back_second = exchange(dq_second)
    grad_keys, grad_values = unpack_keys(
        mine_one, [piece for slab in slabs for piece in (slab, over(slab))]
    )
    early = unpack_queries(back_first, 0, tokens)
    grad_queries = unpack_queries(back_second, 1, tokens, early)
    held = (glob_owner // heads == half)[:, None]
    glob_parts = lax.all_gather(
        jnp.where(held, dglob, 0.0).astype(jnp.bfloat16), "seq", axis=0, tiled=False
    ).astype(jnp.float32)
    glob_sum = (glob_parts[:heads] + glob_parts[heads:]).reshape(heads, G, 2, HD)
    glob_grads = jnp.transpose(glob_sum, (2, 1, 0, 3)).reshape(2, G, features).astype(jnp.bfloat16)
    return (grad_queries, grad_keys, grad_values, glob_grads[0], glob_grads[1])


def body(queries, *rest):
    tokens, features = queries.shape
    blocks = sum(some for _, some in CHUNKS)
    if lax.axis_size("seq") == 2 * (features // HD) and tokens == blocks * BLK:
        return body_halves(queries, *rest)
    return body_shared(queries, *rest)


def solution(mesh):
    return jax.shard_map(
        body,
        mesh=mesh,
        in_specs=(
            P("seq", "tp"),
            P("seq", "tp"),
            P("seq", "tp"),
            P("seq", "tp"),
            P("seq", "tp"),
            P("tp", "seq"),
            P("seq", None, "tp"),
            P("seq", None, "tp"),
            P(),
            P(),
        ),
        out_specs=(P("seq", "tp"), P("seq", "tp"), P("seq", "tp"), P(None, "tp"), P(None, "tp")),
        check_vma=False,
    )
```
